32 devices in a mesh: shard: 2 (over y), tensor: 4 (over x, core), section: 4 (over z).
Axes of the slice: x: 2, y: 2, z: 4, core: 2. Of those that a mesh axis runs over, the one named last changes fastest.
Arguments:
- grad_parts: float32 [2, 4, 4, 1152, 1024], P('shard', 'tensor', 'section'), may hold values from -1 to 1
- master: float32 [1152, 16, 1024], P(('tensor', 'section'), 'shard'), may hold values from -0.1875 to 0.1875
- owner_map: int32 [4, 4], replicated, may hold values from 0 to 1, as said below
- left_factor: float32 [16, 1152, 1152], P('shard', ('tensor', 'section')), may hold values from -1.2 to 11.2, as said below
- right_factor: float32 [16, 1024, 1024], P('shard', ('tensor', 'section')), may hold values from -1.2 to 11.2, as said below
- left_basis: float32 [16, 1152, 1152], P('shard', ('tensor', 'section')), may hold values from -0.1875 to 0.1875
- right_basis: float32 [16, 1024, 1024], P('shard', None, ('tensor', 'section')), may hold values from -0.1875 to 0.1875
- moment_one: float32 [16, 1152, 1024], P('shard', ('tensor', 'section')), may hold values from -3 to 3
- moment_two: float32 [16, 1152, 1024], P('shard', ('tensor', 'section')), may hold values from 0.01 to 0.5
Outputs:
- new_master: float32 [1152, 16, 1024], P(('tensor', 'section'), 'shard')
- update_dir: float32 [1152, 16, 1024], P(('tensor', 'section'), 'shard')
- new_left: float32 [16, 1152, 1152], P('shard', ('tensor', 'section'))
- new_right: float32 [16, 1024, 1024], P('shard', ('tensor', 'section'))
- new_moment_one: float32 [16, 1152, 1024], P('shard', ('tensor', 'section'))
- new_moment_two: float32 [16, 1152, 1024], P('shard', ('tensor', 'section'))
The draws below stay inside these ranges and needn't reach their ends.
Inputs may be any that keep to these rules, and one draw needn't show every extreme that they name: `owner_map`: each shard index owns exactly 8 matrices. `left_factor`: symmetric in its last two dimensions. `right_factor`: symmetric in its last two dimensions.
All inputs are finite; a program needn't handle non-finite values.
Results may differ from the reference program's by a relative error of at most 0.0003.
Values sent between devices are 32-bit elements; how exact they have to be, the bound alone decides.
A program may use at most 448 MiB of HBM per device.

```python
import math
import jax
import jax.numpy as jnp
from jax import lax

D = 1024
BLOCK = 1152
BLOCKS = 4
LAYERS = 4
MATS = 16
OWN = 8
N_SHARD = 2


def symmetric_draw(key, number, extent):
    key_one, key_two = jax.random.split(key)
    noise_draw = jax.random.truncated_normal(key_one, -4.0, 4.0, (number, extent, extent), jnp.float32)
    symmetric = 0.5 * (noise_draw + jnp.swapaxes(noise_draw, 1, 2))
    diagonal = jnp.exp(jax.random.uniform(key_two, (number, 1, extent), jnp.float32, 0.0, 2.3))
    identity = (jnp.arange(extent)[:, None] == jnp.arange(extent)[None, :]).astype(jnp.float32)
    return 0.3 * symmetric + diagonal * identity


def draw_left_factor(key, part):
    return symmetric_draw(jax.random.fold_in(key, 11), MATS, BLOCK)


def draw_right_factor(key, part):
    return symmetric_draw(jax.random.fold_in(key, 23), MATS, D)


def draw_owner_map(key, part):
    shuffled = jax.random.permutation(jax.random.fold_in(key, 37), MATS).astype(jnp.int32)
    return (shuffled // OWN).astype(jnp.int32).reshape(BLOCKS, LAYERS)


def spiked(drawn, key, source, target, parts, factor):
    def block_of(axis_at):
        return (jnp.arange(drawn.shape[axis_at]) // (drawn.shape[axis_at] // parts)).reshape((-1,) + (1,) * (drawn.ndim - 1 - axis_at))

    one_side = jax.random.permutation(key, parts)[block_of(target)]
    far = (block_of(target) + parts // 2) % parts
    return jnp.where((block_of(source) == one_side) | (block_of(source) == far), factor * drawn, drawn)


def levels(key, shape, cuts, low, high):
    level = 1.0
    for position, parts in cuts:
        steps = jax.random.uniform(jax.random.fold_in(jax.random.fold_in(key, 6), position), (parts,), jnp.float32, low / len(cuts), high / len(cuts))
        level = level * jnp.repeat(jnp.exp(steps), shape[position] // parts).reshape((-1,) + (1,) * (len(shape) - 1 - position))
    return level


def noise(own_key, shape, deviation, reach, cuts=(), held_as=jnp.bfloat16):
    result = deviation * jax.random.normal(own_key, shape, jnp.float32)
    if cuts:
        result = result * levels(own_key, shape, cuts, -0.22, 0.18)
    return jnp.clip(result, -reach, reach).astype(held_as)


def noise_with(stream_key, shape, deviation, most, cuts, heavy, held_as=jnp.bfloat16):
    entries = deviation * jax.random.normal(stream_key, shape, jnp.float32)
    if cuts:
        entries = entries * levels(stream_key, shape, cuts, -0.22, 0.18)
    return jnp.clip(spiked(entries, jax.random.fold_in(stream_key, 3), *heavy), -most, most).astype(held_as)


def setup_inputs(seed: int = 0) -> dict:
    splits = jax.random.split(jax.random.key(seed), 10)
    grad_parts = noise_with(splits[0], (N_SHARD, BLOCKS, LAYERS, BLOCK, D), 0.045, 1.0, ((0, 2), (1, 4), (2, 4)), (0, 3, 2, 2.0), jnp.float32)
    master = noise(splits[1], (BLOCK, MATS, D), BLOCK ** -0.5, 0.1875, ((0, 16), (1, 2)), jnp.float32)
    owner_map = draw_owner_map(jax.random.fold_in(splits[9], 71), 0)
    left_factor = draw_left_factor(jax.random.fold_in(splits[9], 71), 0)
    right_factor = draw_right_factor(jax.random.fold_in(splits[9], 71), 0)
    left_basis = noise(splits[5], (MATS, BLOCK, BLOCK), BLOCK ** -0.5, 0.1875, ((0, 2), (1, 16)), jnp.float32)
    right_basis = noise(splits[6], (MATS, D, D), D ** -0.5, 0.1875, ((0, 2), (2, 16)), jnp.float32)
    moment_one = noise(splits[7], (MATS, BLOCK, D), 0.2, 3.0, ((0, 2), (1, 16)), jnp.float32)
    moment_two = jnp.clip(jnp.exp(math.log(0.5) - 3.912023 * jax.random.uniform(splits[8], (MATS, BLOCK, D), jnp.float32) ** levels(splits[8], (MATS, BLOCK, D), ((0, 2), (1, 16)), -0.2, 0.2)), 0.01, 0.5)
    return {"grad_parts": grad_parts, "master": master, "owner_map": owner_map, "left_factor": left_factor, "right_factor": right_factor, "left_basis": left_basis, "right_basis": right_basis, "moment_one": moment_one, "moment_two": moment_two}


beta_one = 0.95
beta_two = 0.95
epsilon = 1e-08
learn_rate = 0.01
decay_weight = 0.1
step_count = 10

def slot_table(owner_map, shards):
    owners_flat = owner_map.reshape(-1).astype(jnp.int32)
    matrices = owners_flat.shape[0]
    per_owner = matrices // shards
    member = (owners_flat[:, None] == jnp.arange(shards, dtype=jnp.int32)[None, :]).astype(jnp.int32)
    before = jnp.cumsum(member, axis=0) - member
    rank_in = lax.optimization_barrier(jnp.sum(before * member, axis=1)).astype(jnp.int32)
    slot_of = owners_flat * per_owner + rank_in
    places = (slot_of[:, None] == jnp.arange(matrices, dtype=jnp.int32)[None, :]).astype(jnp.int32)
    source = lax.optimization_barrier(jnp.sum(places * jnp.arange(matrices, dtype=jnp.int32)[:, None], axis=0)).astype(jnp.int32)
    return (slot_of, source)

def reference(grad_parts, master, owner_map, left_factor, right_factor, left_basis, right_basis, moment_one, moment_two):
    exact_mode = lax.Precision.HIGHEST
    summed = lax.optimization_barrier(jnp.sum(grad_parts, axis=0))
    matrices = summed.reshape(MATS, BLOCK, D)
    slot_of, source = slot_table(owner_map, N_SHARD)
    slot_grads = jnp.take(matrices, source, axis=0)
    new_left = beta_two * left_factor + (1.0 - beta_two) * jnp.einsum('qfn,qkn->qfk', slot_grads, slot_grads, precision=exact_mode)
    new_right = beta_two * right_factor + (1.0 - beta_two) * jnp.einsum('qfc,qfn->qcn', slot_grads, slot_grads, precision=exact_mode)
    turned = jnp.einsum('qrf,qfn->qrn', left_basis, slot_grads, precision=exact_mode)
    rotated = jnp.einsum('qrn,qnk->qrk', turned, right_basis, precision=exact_mode)
    new_moment_one = beta_one * moment_one + (1.0 - beta_one) * rotated
    new_moment_two = beta_two * moment_two + (1.0 - beta_two) * rotated * rotated
    first_fix = 1.0 - beta_one ** step_count
    second_fix = 1.0 - beta_two ** step_count
    scaled = new_moment_one / first_fix / (jnp.sqrt(new_moment_two / second_fix) + epsilon)
    pulled = jnp.einsum('qrn,qkn->qrk', scaled, right_basis, precision=exact_mode)
    update = jnp.einsum('qrf,qrk->fqk', left_basis, pulled, precision=exact_mode)
    new_master = master - learn_rate * (update + decay_weight * master)
    return (new_master, update, new_left, new_right, new_moment_one, new_moment_two)
```

```python
import jax
import jax.numpy as jnp
from jax import lax
from jax.sharding import PartitionSpec as P

beta_one = 0.95
beta_two = 0.95
epsilon = 1e-08
learn_rate = 0.01
decay_weight = 0.1
step_count = 10


def slot_table(owner_map, shards):
    owners_flat = owner_map.reshape(-1)
    matrices = owners_flat.shape[0]
    per_owner = matrices // shards
    member = (owners_flat[:, None] == jnp.arange(shards, dtype=jnp.int32)[None, :]).astype(
        jnp.int32
    )
    order = jnp.arange(matrices, dtype=jnp.int32)
    earlier = (order[:, None] > order[None, :]).astype(jnp.int32)
    before = jnp.sum(earlier[:, :, None] * member[None, :, :], axis=1)
    rank_in = jnp.sum(before * member, axis=1)
    slot_of = owners_flat * per_owner + rank_in
    places = (slot_of[:, None] == jnp.arange(matrices, dtype=jnp.int32)[None, :]).astype(jnp.int32)
    source = jnp.sum(places * jnp.arange(matrices, dtype=jnp.int32)[:, None], axis=0)
    return (slot_of, source)


def pick(stacked, indices):
    return jnp.stack(
        [
            lax.dynamic_index_in_dim(stacked, indices[i], 0, keepdims=False)
            for i in range(indices.shape[0])
        ]
    )


def local(
    grad_parts,
    master,
    owner_map,
    left_factor,
    right_factor,
    left_basis,
    right_basis,
    moment_one,
    moment_two,
):
    exact_mode = lax.Precision.HIGHEST
    shards = lax.axis_size("shard")
    members = lax.axis_size(("tensor", "section"))
    position = lax.axis_index(("tensor", "section"))
    slot_of, source = slot_table(owner_map, shards)
    height = left_basis.shape[2]
    width = right_basis.shape[1]
    row_block = height // members
    col_block = width // members
    local_part = grad_parts[0, 0, 0]
    row_piece = lax.psum_scatter(local_part, "shard", scatter_dimension=0, tiled=True)
    stacked = lax.all_gather(row_piece[None], ("tensor", "section"), axis=0, tiled=True)
    ordered = pick(stacked, source)
    full_grad = lax.all_to_all(ordered, "shard", split_axis=0, concat_axis=1, tiled=True)
    full_right = lax.all_gather(right_basis, ("tensor", "section"), axis=2, tiled=True)
    grad_band = lax.dynamic_slice_in_dim(full_grad, position * row_block, row_block, 1)
    grad_slab = lax.dynamic_slice_in_dim(full_grad, position * col_block, col_block, 2)
    new_left = beta_two * left_factor + (1.0 - beta_two) * jnp.einsum(
        "orn,ofn->orf", grad_band, full_grad, precision=exact_mode
    )
    new_right = beta_two * right_factor + (1.0 - beta_two) * jnp.einsum(
        "ofc,ofn->ocn", grad_slab, full_grad, precision=exact_mode
    )
    turned = jnp.einsum("orf,ofn->orn", left_basis, full_grad, precision=exact_mode)
    rotated = jnp.einsum("orn,onk->ork", turned, full_right, precision=exact_mode)
    new_moment_one = beta_one * moment_one + (1.0 - beta_one) * rotated
    new_moment_two = beta_two * moment_two + (1.0 - beta_two) * rotated * rotated
    first_fix = 1.0 - beta_one**step_count
    second_fix = 1.0 - beta_two**step_count
    scaled = new_moment_one / first_fix / (jnp.sqrt(new_moment_two / second_fix) + epsilon)
    pulled = jnp.einsum("orn,okn->ork", scaled, full_right, precision=exact_mode)
    update_dir = lax.psum_scatter(
        jnp.einsum("orf,ork->fok", left_basis, pulled, precision=exact_mode),
        ("tensor", "section"),
        scatter_dimension=0,
        tiled=True,
    )
    new_master = master - learn_rate * (update_dir + decay_weight * master)
    return (new_master, update_dir, new_left, new_right, new_moment_one, new_moment_two)


def slotwise(
    grad_parts,
    master,
    owner_map,
    left_factor,
    right_factor,
    left_basis,
    right_basis,
    moment_one,
    moment_two,
):
    mode = lax.Precision.HIGH
    group = ("major", "section")
    everyone = ("major", "minor", "section")
    shards = lax.axis_size("shard")
    majors = lax.axis_size("major")
    sections = lax.axis_size("section")
    members = 2 * majors * sections
    slots = members // 2
    side = lax.axis_index("minor")
    _, source = slot_table(owner_map, shards)
    height = left_basis.shape[2]
    width = right_basis.shape[1]
    rows = height // members
    cols = width // members
    part = width // shards

    def swap(bands):
        return lax.all_to_all(bands, group, split_axis=0, concat_axis=0, tiled=True)

    def across(axis, value):
        return lax.ppermute(value, axis, [(0, 1), (1, 0)])

    def in_order(index, own, other, axis):
        lower = jnp.where(index == 0, own, other)
        upper = jnp.where(index == 0, other, own)
        return jnp.stack((lower, upper), axis=axis)

    def natural(own, other):
        shape = (majors, sections) + own.shape[1:]
        return in_order(side, own.reshape(shape), other.reshape(shape), 1)

    me = lax.axis_index("shard")
    partial = grad_parts[0, 0, 0]
    kept = lax.dynamic_slice_in_dim(partial, me * part, part, 1)
    crossing = across("shard", lax.dynamic_slice_in_dim(partial, (1 - me) * part, part, 1))
    left_half = swap(left_basis)
    crossing, left_half = lax.optimization_barrier((crossing, left_half))
    summed = kept + crossing
    pieces = lax.all_to_all(
        summed.reshape(members, rows, part), everyone, split_axis=0, concat_axis=0, tiled=True
    )
    right_bands = jnp.swapaxes(right_basis, 1, 2)
    pieces, right_bands = lax.optimization_barrier((pieces, right_bands))
    theirs = pick(pieces, lax.dynamic_slice_in_dim(source, (1 - me) * slots, slots))
    ours = pick(pieces, lax.dynamic_slice_in_dim(source, me * slots, slots))
    arrived = across("shard", theirs)
    right_half = swap(right_bands)
    arrived, right_half = lax.optimization_barrier((arrived, right_half))
    bands = swap(in_order(me, ours, arrived, 1))
    whole = natural(bands, across("minor", bands))
    grad = jnp.swapaxes(whole, 3, 4).reshape(height, width)
    right_turned = natural(right_half, across("minor", right_half)).reshape(width, width)
    left_other = across("minor", left_half).reshape(height // 2, height)
    left_half = left_half.reshape(height // 2, height)

    turned = jnp.einsum("rf,fn->rn", left_half, grad, precision=mode)
    rotated_half = jnp.einsum("rn,kn->rk", turned, right_turned, precision=mode)
    band_rows = lax.dynamic_index_in_dim(
        grad.reshape(majors, 2, sections * rows, width), side, 1, keepdims=False
    ).reshape(height // 2, width)
    left_product = jnp.einsum("rn,fn->rf", band_rows, grad, precision=mode)
    band_cols = lax.dynamic_index_in_dim(
        grad.reshape(height, majors, 2, sections * cols), side, 2, keepdims=False
    ).reshape(height, width // 2)
    right_product = jnp.einsum("fc,fn->cn", band_cols, grad, precision=mode)
    rotated = swap(rotated_half.reshape(slots, rows, width))
    rotated, left_product, right_product = lax.optimization_barrier(
        (rotated, left_product, right_product)
    )
    new_moment_one = beta_one * moment_one + (1.0 - beta_one) * rotated
    new_moment_two = beta_two * moment_two + (1.0 - beta_two) * rotated * rotated
    first_fix = 1.0 - beta_one**step_count
    second_fix = 1.0 - beta_two**step_count
    scaled = new_moment_one / first_fix / (jnp.sqrt(new_moment_two / second_fix) + epsilon)
    scaled_half = swap(scaled).reshape(height // 2, width)

    new_left = beta_two * left_factor + (1.0 - beta_two) * swap(
        left_product.reshape(slots, rows, height)
    )
    new_right = beta_two * right_factor + (1.0 - beta_two) * swap(
        right_product.reshape(slots, cols, width)
    )

    pulled_half = jnp.einsum("rk,kn->rn", scaled_half, right_turned, precision=mode)
    pulled_other = across("minor", pulled_half)

    def my_columns(half):
        split = half.reshape(height // 2, majors, 2, sections * rows)
        return lax.dynamic_index_in_dim(split, side, 2, keepdims=False).reshape(
            height // 2, height // 2
        )

    update_half = jnp.einsum(
        "rf,rn->fn", my_columns(left_half), pulled_half, precision=mode
    ) + jnp.einsum("rf,rn->fn", my_columns(left_other), pulled_other, precision=mode)
    update_dir = jnp.swapaxes(swap(update_half.reshape(slots, rows, width)), 0, 1)
    new_master = master - learn_rate * (update_dir + decay_weight * master)
    return (new_master, update_dir, new_left, new_right, new_moment_one, new_moment_two)


def solution(mesh):
    shards, tensors, sections = (mesh.shape[name] for name in ("shard", "tensor", "section"))

    def run(*operands):
        own = operands[3].shape[0] // shards
        paired = shards == 2 and tensors % 2 == 0 and 2 * own == tensors * sections
        if paired:
            shape = (shards, tensors // 2, 2, sections)
            grid = jax.sharding.Mesh(
                mesh.devices.reshape(shape), ("shard", "major", "minor", "section")
            )
            body, tensor = slotwise, ("major", "minor")
        else:
            grid, body, tensor = mesh, local, ("tensor",)
        band = tensor + ("section",)
        placed = (
            P("shard", tensor, "section", None, None),
            P(band, "shard", None),
            P(),
            P("shard", band, None),
            P("shard", band, None),
            P("shard", band, None),
            P("shard", None, band),
            P("shard", band, None),
            P("shard", band, None),
        )
        results = (placed[1], placed[1], placed[3], placed[4], placed[7], placed[8])
        return jax.shard_map(
            body, mesh=grid, in_specs=placed, out_specs=results, check_vma=False
        )(*operands)

    return run
```

```python
import jax
import jax.numpy as jnp
from jax import lax
from jax.experimental import pallas as pl
from jax.experimental.pallas import tpu as pltpu
from jax.sharding import PartitionSpec as P

beta_one = 0.95
beta_two = 0.95
epsilon = 1e-08
learn_rate = 0.01
decay_weight = 0.1
step_count = 10


def slot_table(owner_map, shards):
    owners_flat = owner_map.reshape(-1)
    matrices = owners_flat.shape[0]
    per_owner = matrices // shards
    member = (owners_flat[:, None] == jnp.arange(shards, dtype=jnp.int32)[None, :]).astype(
        jnp.int32
    )
    order = jnp.arange(matrices, dtype=jnp.int32)
    earlier = (order[:, None] > order[None, :]).astype(jnp.int32)
    before = jnp.sum(earlier[:, :, None] * member[None, :, :], axis=1)
    rank_in = jnp.sum(before * member, axis=1)
    slot_of = owners_flat * per_owner + rank_in
    places = (slot_of[:, None] == jnp.arange(matrices, dtype=jnp.int32)[None, :]).astype(jnp.int32)
    source = jnp.sum(places * jnp.arange(matrices, dtype=jnp.int32)[:, None], axis=0)
    return (slot_of, source)


def pick(stacked, indices):
    return jnp.stack(
        [
            lax.dynamic_index_in_dim(stacked, indices[i], 0, keepdims=False)
            for i in range(indices.shape[0])
        ]
    )


def local(
    grad_parts,
    master,
    owner_map,
    left_factor,
    right_factor,
    left_basis,
    right_basis,
    moment_one,
    moment_two,
):
    exact_mode = lax.Precision.HIGHEST
    shards = lax.axis_size("shard")
    members = lax.axis_size(("tensor", "section"))
    position = lax.axis_index(("tensor", "section"))
    slot_of, source = slot_table(owner_map, shards)
    height = left_basis.shape[2]
    width = right_basis.shape[1]
    row_block = height // members
    col_block = width // members
    local_part = grad_parts[0, 0, 0]
    row_piece = lax.psum_scatter(local_part, "shard", scatter_dimension=0, tiled=True)
    stacked = lax.all_gather(row_piece[None], ("tensor", "section"), axis=0, tiled=True)
    ordered = pick(stacked, source)
    full_grad = lax.all_to_all(ordered, "shard", split_axis=0, concat_axis=1, tiled=True)
    full_right = lax.all_gather(right_basis, ("tensor", "section"), axis=2, tiled=True)
    grad_band = lax.dynamic_slice_in_dim(full_grad, position * row_block, row_block, 1)
    grad_slab = lax.dynamic_slice_in_dim(full_grad, position * col_block, col_block, 2)
    new_left = beta_two * left_factor + (1.0 - beta_two) * jnp.einsum(
        "orn,ofn->orf", grad_band, full_grad, precision=exact_mode
    )
    new_right = beta_two * right_factor + (1.0 - beta_two) * jnp.einsum(
        "ofc,ofn->ocn", grad_slab, full_grad, precision=exact_mode
    )
    turned = jnp.einsum("orf,ofn->orn", left_basis, full_grad, precision=exact_mode)
    rotated = jnp.einsum("orn,onk->ork", turned, full_right, precision=exact_mode)
    new_moment_one = beta_one * moment_one + (1.0 - beta_one) * rotated
    new_moment_two = beta_two * moment_two + (1.0 - beta_two) * rotated * rotated
    first_fix = 1.0 - beta_one**step_count
    second_fix = 1.0 - beta_two**step_count
    scaled = new_moment_one / first_fix / (jnp.sqrt(new_moment_two / second_fix) + epsilon)
    pulled = jnp.einsum("orn,okn->ork", scaled, full_right, precision=exact_mode)
    update_dir = lax.psum_scatter(
        jnp.einsum("orf,ork->fok", left_basis, pulled, precision=exact_mode),
        ("tensor", "section"),
        scatter_dimension=0,
        tiled=True,
    )
    new_master = master - learn_rate * (update_dir + decay_weight * master)
    return (new_master, update_dir, new_left, new_right, new_moment_one, new_moment_two)


def halves(value):
    high = value.astype(jnp.bfloat16)
    return high, (value - high.astype(jnp.float32)).astype(jnp.bfloat16)


def triple(first, second, contract):
    def one(a, b):
        return lax.dot_general(a, b, (contract, ((), ())), preferred_element_type=jnp.float32)

    (a, a_low), (b, b_low) = first, second
    return one(a, b) + (one(a, b_low) + one(a_low, b))


PLAIN = ((1,), (0,))
TURNED = ((1,), (1,))
CHUNKS = 4


def banded(
    grad,
    source,
    left,
    right,
    old_one,
    old_two,
    left_out,
    right_out,
    update_out,
    one_out,
    two_out,
    cross,
    pieces,
    full_grad,
    left_half,
    right_full,
    turned_in,
    scaled_in,
    update_in,
    summed,
    crossed,
    piece,
    load,
    load_left,
    g_hi,
    g_lo,
    gt_hi,
    gt_lo,
    l_hi,
    l_lo,
    lt_hi,
    lt_lo,
    r_hi,
    r_lo,
    p_hi,
    p_lo,
    q_hi,
    q_lo,
    update,
    left_prod,
    right_prod,
    one,
    two,
    scaled,
    local_sem,
    cross_send,
    cross_recv,
    band_send,
    band_recv,
    mirror_send,
    mirror_recv,
    pick_send,
    pick_recv,
    left_send,
    left_recv,
    right_send,
    right_recv,
    relay_send,
    relay_recv,
    turned_send,
    turned_recv,
    scaled_send,
    scaled_recv,
    update_send,
    update_recv,
    final_send,
    final_recv,
):
    mesh_id = pl.DeviceIdType.MESH
    y, b, z = lax.axis_index("shard"), lax.axis_index("tensor"), lax.axis_index("section")
    h, zin = lax.div(z, 2), lax.rem(z, 2)
    core_z = 1 + h
    inner = (z == 1) | (z == 2)
    rows, height = left.shape[1], left.shape[2]
    cols, width = right.shape[1], right.shape[2]
    half = width // 2
    band = 4 * rows
    pair, wide = 2 * rows, 2 * cols
    tile = min(256, half)
    tiles = width // tile
    tall = 384 if height % 384 == 0 else 128

    def within(start, size, unit=8):
        return pl.ds(pl.multiple_of(start, unit), size)

    def copy(src, dst, send, recv, target):
        return pltpu.make_async_remote_copy(
            src_ref=src,
            dst_ref=dst,
            send_sem=send,
            recv_sem=recv,
            device_id=target,
            device_id_type=mesh_id,
        )

    def give(src, dst, send, recv, target):
        here = (target[0] == y) & (target[1] == b) & (target[2] == z)

        @pl.when(here)
        def _():
            pltpu.make_async_copy(src, dst, send).start()

        @pl.when(jnp.logical_not(here))
        def _():
            copy(src, dst, send, recv, target).start()

    def took(ref, sem):
        pltpu.make_async_copy(ref, ref, sem).wait()

    def fetch(src, dst):
        moved = pltpu.make_async_copy(src, dst, local_sem)
        moved.start()
        moved.wait()

    def fetch_all(moves, whole):
        for src, dst in moves:
            pltpu.make_async_copy(src, dst, local_sem).start()
        took(whole, local_sem)

    def loop(count, body):
        def run(i, carry):
            body(i)
            return carry

        lax.fori_loop(0, count, run, 0)

    barrier = pltpu.get_barrier_semaphore()
    for dy in range(2):
        for db in range(4):
            for dz in range(2):
                if dy or db or dz:
                    other = (
                        lax.rem(y + dy, 2),
                        lax.rem(b + db, 4),
                        2 * h + lax.rem(zin + dz, 2),
                    )
                    pl.semaphore_signal(barrier, inc=1, device_id=other, device_id_type=mesh_id)

    @pl.when(inner)
    def _():
        pl.semaphore_signal(barrier, inc=1, device_id=(y, b, 3 - z), device_id_type=mesh_id)
        pl.semaphore_wait(barrier, 16)

    @pl.when(jnp.logical_not(inner))
    def _():
        pl.semaphore_wait(barrier, 15)

    def lanes(side):
        return within(side * half, half, 128)

    for s in range(CHUNKS):
        copy(
            grad.at[:, pl.ds(s * rows, rows), lanes(1 - y)],
            cross.at[s],
            cross_send.at[s],
            cross_recv.at[s],
            (1 - y, b, z),
        ).start()

    def send_right(w):
        for t in range(4):
            give(
                right.at[4 * w + t],
                right_full.at[w, b, h, within(zin * cols, cols)],
                right_send.at[w, t],
                right_recv.at[w],
                (y, t, core_z),
            )

    def send_left(w):
        for t in range(4):
            give(
                left.at[4 * w + t],
                left_half.at[w, b, within(zin * rows, rows)],
                left_send.at[w, t],
                left_recv.at[w],
                (y, t, core_z),
            )

    def drain_right(w):
        for t in range(4):
            took(right.at[0], right_send.at[w, t])

    def drain_left(w):
        for t in range(4):
            took(left.at[0], left_send.at[w, t])

    def drain_bands(s):
        for t in range(4):
            took(summed.at[s, t], band_send.at[s, t])

    def drain_scaled(w):
        for t in range(4):
            took(scaled.at[t], scaled_send.at[w, t])

    def relay_right(w):
        drain_right(w)
        took(right.at[pl.ds(0, 7)], right_recv.at[w])
        copy(
            right_full.at[w, :, h],
            right_full.at[w, :, h],
            relay_send.at[w],
            relay_recv.at[w],
            (y, b, 3 - z),
        ).start()

    def sum_stage(s):
        fetch(grad.at[:, pl.ds(s * rows, rows), lanes(y)], summed.at[s])
        took(cross.at[s], cross_recv.at[s])
        fetch(cross.at[s], crossed)
        summed[s] = summed[s] + crossed[...]
        for t in range(4):
            give(
                summed.at[s, t],
                pieces.at[s, b, h, zin],
                band_send.at[s, t],
                band_recv.at[s],
                (y, t, core_z),
            )

    def mirror_stage(s):
        drain_bands(s)
        took(full_grad.at[0, pl.ds(0, 7), pl.ds(0, rows)], band_recv.at[s])
        copy(
            pieces.at[s, :, h],
            pieces.at[s, :, h],
            mirror_send.at[s],
            mirror_recv.at[s],
            (y, b, 3 - z),
        ).start()

    def staged(s, o, t, w):
        return update.at[s % 2, pl.ds((4 * o + t) * rows, rows), pl.ds(w * half, half)]

    def drain_pick(s):
        for o in range(2):
            for t in range(4):
                for w in range(2):
                    took(staged(s, o, t, w), pick_send.at[s, o, t, w])

    def pick_stage(s):
        took(pieces.at[s, :, 1 - h], mirror_recv.at[s])
        fetch(pieces.at[s], piece)
        if s >= 2:
            drain_pick(s - 2)
        for o in range(2):
            for t in range(4):
                for w in range(2):
                    at = 8 * o + 4 * w + t
                    block = staged(s, o, t, w)
                    block[...] = piece[source[0, at], source[1, at], source[2, at]]
                    give(
                        block,
                        full_grad.at[w, 4 * y + b, pl.ds(s * rows, rows)],
                        pick_send.at[s, o, t, w],
                        pick_recv.at[0],
                        (o, t, z),
                    )

    def gather_gradients():
        send_right(0)
        later = {1: lambda: send_left(0), 2: lambda: send_right(1), 3: lambda: send_left(1)}
        for s in range(CHUNKS):
            sum_stage(s)
            if s in later:
                later[s]()

            @pl.when(inner)
            def _():
                if s == 1:
                    relay_right(0)
                if s >= 1:
                    mirror_stage(s - 1)
                if s >= 2:
                    pick_stage(s - 2)

    def prepare(w):
        fetch_all(
            [
                (
                    full_grad.at[w, 4 * side + t],
                    load.at[pl.ds(t * band, band), pl.ds(side * half, half)],
                )
                for side in range(2)
                for t in range(4)
            ],
            full_grad.at[w],
        )

        def by_rows(i):
            at = within(i * pair, pair, 16)
            high, low = halves(load[at, :])
            for side in range(2):
                g_hi[side, at, :] = high[:, side * half : (side + 1) * half]
                g_lo[side, at, :] = low[:, side * half : (side + 1) * half]

        loop(8, by_rows)

        def by_columns(t):
            own = load[pl.ds(0, height), within((2 * t + h) * wide, wide, wide)]
            high, low = halves(own.T)
            at = within(t * wide, wide, 16)
            gt_hi[at, :] = high
            gt_lo[at, :] = low

        loop(4, by_columns)

    def prepare_left(w):
        drain_left(w)
        took(left.at[pl.ds(0, 7)], left_recv.at[w])
        fetch_all(
            [(left_half.at[w, t], load_left.at[pl.ds(t * pair, pair)]) for t in range(4)],
            left_half.at[w],
        )

        def by_rows(t):
            at = within(t * pair, pair, 16)
            high, low = halves(load_left[at, :])
            l_hi[at, :] = high
            l_lo[at, :] = low

        loop(4, by_rows)

        def by_columns(i):
            at = within(i * 128, 128, 128)
            high, low = halves(load_left[:, at].T)
            lt_hi[w, at, :] = high
            lt_lo[w, at, :] = low

        loop(height // 128, by_columns)

    def prepare_right(w):
        took(right_full.at[w, :, 1 - h], relay_recv.at[w])
        fetch_all(
            [
                (right_full.at[w, t, v], load.at[pl.ds((2 * t + v) * wide, wide)])
                for t in range(4)
                for v in range(2)
            ],
            right_full.at[w],
        )

        def by_rows(i):
            at = within(i * wide, wide, 16)
            high, low = halves(load[at, :])
            r_hi[w, at, :] = high
            r_lo[w, at, :] = low

        loop(8, by_rows)

    def turn(w):
        for m in range(2):
            at = pl.ds(m * band, band)

            def body(n):
                side, spot = n // (tiles // 2), within(n % (tiles // 2) * tile, tile, tile)
                product = triple(
                    (l_hi[at, :], l_lo[at, :]),
                    (g_hi[side, :, spot], g_lo[side, :, spot]),
                    PLAIN,
                )
                high, low = halves(product)
                into = within(n * tile, tile, tile)
                p_hi[at, into] = high
                p_lo[at, into] = low

            loop(tiles, body)

    def rotated(t, v):
        return load_left.at[pl.ds(t * pair + v * rows, rows), pl.ds(0, width)]

    def drain_turned(w):
        for t in range(4):
            for v in range(2):
                took(rotated(t, v), turned_send.at[w, t, v])

    def rotate(w):
        for m in range(2):
            at = pl.ds(m * band, band)

            def body(n):
                spot = within(n * tile, tile, tile)
                load_left[at, spot] = triple(
                    (p_hi[at, :], p_lo[at, :]), (r_hi[w, spot, :], r_lo[w, spot, :]), TURNED
                )

            loop(tiles, body)
            for t in (2 * m, 2 * m + 1):
                for v in range(2):
                    give(
                        rotated(t, v),
                        turned_in.at[w, b],
                        turned_send.at[w, t, v],
                        turned_recv.at[w],
                        (y, t, 2 * h + v),
                    )

    def drain_products(w):
        for t in range(4):
            for v in range(2):
                took(left_prod.at[pl.ds(0, rows)], final_send.at[0, w, t, v])
                took(right_prod.at[pl.ds(0, cols)], final_send.at[1, w, t, v])

    def products(w):
        if w:
            drain_products(w - 1)
        for m in range(2):
            at = pl.ds(m * band, band)
            spots = [within(t * band + h * pair, pair, 16) for t in (2 * m, 2 * m + 1)]

            def body(n):
                spot = within(n * tall, tall, 128)
                total = None
                for side in range(2):
                    own = [
                        jnp.concatenate([g[side, one_spot, :] for one_spot in spots], axis=0)
                        for g in (g_hi, g_lo)
                    ]
                    product = triple(own, (g_hi[side, spot, :], g_lo[side, spot, :]), TURNED)
                    total = product if total is None else total + product
                left_prod[at, spot] = total

            loop(height // tall, body)
            for t in (2 * m, 2 * m + 1):
                for v in range(2):
                    give(
                        left_prod.at[pl.ds(t * pair + v * rows, rows)],
                        left_out.at[4 * w + b],
                        final_send.at[0, w, t, v],
                        final_recv.at[0],
                        (y, t, 2 * h + v),
                    )
        for m in range(2):
            at = pl.ds(m * 2 * wide, 2 * wide)

            def body(n):
                side, spot = n // (tiles // 2), within(n % (tiles // 2) * tile, tile, tile)
                right_prod[at, within(n * tile, tile, tile)] = triple(
                    (gt_hi[at, :], gt_lo[at, :]),
                    (g_hi[side, :, spot], g_lo[side, :, spot]),
                    PLAIN,
                )

            loop(tiles, body)
            for t in (2 * m, 2 * m + 1):
                for v in range(2):
                    give(
                        right_prod.at[pl.ds(t * wide + v * cols, cols)],
                        right_out.at[4 * w + b],
                        final_send.at[1, w, t, v],
                        final_recv.at[1],
                        (y, t, 2 * h + v),
                    )

    def moments(w):
        slots = pl.ds(4 * w, 4)
        fetch_all([(old_one.at[slots], one)], one)
        fetch_all([(old_two.at[slots], two)], two)

        @pl.when(inner)
        def _():
            drain_turned(w)
            took(old_one.at[pl.ds(0, 3)], turned_recv.at[w])

        @pl.when(jnp.logical_not(inner))
        def _():
            took(old_one.at[pl.ds(0, 4)], turned_recv.at[w])

        fetch(turned_in.at[w], scaled)
        first_fix = 1.0 - beta_one**step_count
        second_fix = 1.0 - beta_two**step_count
        for t in range(4):

            def body(i):
                at = within(i * 8, 8)
                value = scaled[t, at, :]
                new_one = beta_one * one[t, at, :] + (1.0 - beta_one) * value
                new_two = beta_two * two[t, at, :] + (1.0 - beta_two) * value * value
                one[t, at, :] = new_one
                two[t, at, :] = new_two
                scaled[t, at, :] = (
                    new_one / first_fix / (jnp.sqrt(new_two / second_fix) + epsilon)
                )

            loop(rows // 8, body)
            give(
                scaled.at[t],
                scaled_in.at[w, b, within(zin * rows, rows)],
                scaled_send.at[w, t],
                scaled_recv.at[w],
                (y, t, core_z),
            )
        fetch(one, one_out.at[slots])
        fetch(two, two_out.at[slots])

    def pull(w):
        took(old_one.at[pl.ds(0, 7)], scaled_recv.at[w])
        fetch_all(
            [(scaled_in.at[w, t], load.at[pl.ds(t * pair, pair)]) for t in range(4)],
            scaled_in.at[w],
        )

        def by_rows(t):
            at = within(t * pair, pair, 16)
            high, low = halves(load[at, :])
            p_hi[at, :] = high
            p_lo[at, :] = low

        loop(4, by_rows)
        for m in range(2):
            at = pl.ds(m * band, band)

            def body(n):
                spot = within(n * tile, tile, tile)
                high, low = halves(
                    triple((p_hi[at, :], p_lo[at, :]), (r_hi[w, :, spot], r_lo[w, :, spot]), PLAIN)
                )
                q_hi[at, spot] = high
                q_lo[at, spot] = low

            loop(tiles, body)

    def mirrored(t):
        return update.at[0, pl.ds(t * pair, pair)]

    def drain_update(w):
        for t in range(4):
            took(mirrored(t), update_send.at[w, t])
            for v in range(2):
                took(update.at[1, pl.ds(0, rows)], final_send.at[2, w, t, v])

    def back(w):
        if w:
            drain_update(w - 1)
        for slot, side in ((0, 1 - h), (1, h)):
            for m in range(2):
                at = pl.ds(m * band, band)
                spots = [within(t * band + side * pair, pair, 16) for t in (2 * m, 2 * m + 1)]

                def body(n):
                    spot = within(n * tile, tile, tile)
                    own = [
                        jnp.concatenate([turned[w, one_spot, :] for one_spot in spots], axis=0)
                        for turned in (lt_hi, lt_lo)
                    ]
                    update[slot, at, spot] = triple(own, (q_hi[:, spot], q_lo[:, spot]), PLAIN)

                loop(tiles, body)
                if slot == 0:
                    for t in (2 * m, 2 * m + 1):
                        copy(
                            mirrored(t),
                            update_in.at[w, t],
                            update_send.at[w, t],
                            update_recv.at[w, t],
                            (y, b, 3 - z),
                        ).start()

    def finish(w):
        for t in range(4):
            took(update_in.at[w, t], update_recv.at[w, t])
            at = pl.ds(t * pair, pair)
            fetch(update_in.at[w, t], load.at[at])
            update[1, at] = update[1, at] + load[at, :]
            for v in range(2):
                give(
                    update.at[1, pl.ds(t * pair + v * rows, rows)],
                    update_out.at[4 * w + b],
                    final_send.at[2, w, t, v],
                    final_recv.at[2],
                    (y, t, 2 * h + v),
                )

    gather_gradients()

    @pl.when(inner)
    def _():
        mirror_stage(CHUNKS - 1)
        relay_right(1)
        for s in (CHUNKS - 2, CHUNKS - 1):
            pick_stage(s)
        for s in (CHUNKS - 2, CHUNKS - 1):
            drain_pick(s)
        took(full_grad.at[:, pl.ds(0, 7)], pick_recv.at[0])
        prepare(0)
        prepare_left(0)
        turn(0)
        prepare_right(0)
        rotate(0)
        products(0)

    moments(0)

    @pl.when(inner)
    def _():
        prepare(1)
        prepare_left(1)
        turn(1)
        prepare_right(1)
        rotate(1)
        drain_scaled(0)
        pull(0)
        back(0)

    @pl.when(jnp.logical_not(inner))
    def _():
        drain_scaled(0)

    moments(1)

    @pl.when(inner)
    def _():
        products(1)
        finish(0)
        drain_scaled(1)
        pull(1)
        back(1)
        finish(1)
        drain_products(1)
        drain_update(1)
        for s in range(CHUNKS):
            took(pieces.at[s, :, h], mirror_send.at[s])
        for w in range(2):
            took(right_full.at[w, :, h], relay_send.at[w])
        took(left.at[pl.ds(0, 6)], final_recv.at[0])
        took(right.at[pl.ds(0, 6)], final_recv.at[1])
        took(old_one.at[pl.ds(0, 6)], final_recv.at[2])

    @pl.when(jnp.logical_not(inner))
    def _():
        for s in range(CHUNKS):
            drain_bands(s)
        for w in range(2):
            drain_left(w)
            drain_right(w)
        drain_scaled(1)
        took(left, final_recv.at[0])
        took(right, final_recv.at[1])
        took(old_one, final_recv.at[2])

    for s in range(CHUNKS):
        took(cross.at[s], cross_send.at[s])


def waved(
    grad_parts,
    master,
    owner_map,
    left_factor,
    right_factor,
    left_basis,
    right_basis,
    moment_one,
    moment_two,
):
    _, source = slot_table(owner_map, lax.axis_size("shard"))
    places = jnp.stack((source // 4, source % 4 // 2, source % 2))
    slots, rows, height = left_basis.shape
    width = right_basis.shape[1]
    cols, half, band, pair, wide = width // 16, width // 2, 4 * rows, 2 * rows, width // 8
    f32, bf16 = jnp.float32, jnp.bfloat16
    right_turned = jnp.swapaxes(right_basis, 1, 2)
    grad = grad_parts[0, 0, 0].reshape(4, band, width)

    def array(*shape):
        return jax.ShapeDtypeStruct(shape, f32)

    def twice(*shape):
        return [pltpu.VMEM(shape, bf16)] * 2

    sems = [
        (CHUNKS,),
        (CHUNKS,),
        (CHUNKS, 4),
        (CHUNKS,),
        (CHUNKS,),
        (CHUNKS,),
        (CHUNKS, 2, 4, 2),
        (1,),
        (2, 4),
        (2,),
        (2, 4),
        (2,),
        (2,),
        (2,),
        (2, 4, 2),
        (2,),
        (2, 4),
        (2,),
        (2, 4),
        (2, 4),
        (3, 2, 4, 2),
        (3,),
    ]
    products = 6 * 2 * 2 * height * height * width
    results = pl.pallas_call(
        banded,
        out_shape=[
            array(slots, rows, height),
            array(slots, cols, width),
            array(slots, rows, width),
            array(slots, rows, width),
            array(slots, rows, width),
            array(CHUNKS, 4, rows, half),
            array(CHUNKS, 4, 2, 2, rows, half),
            array(2, 8, band, half),
            array(2, 4, pair, height),
            array(2, 4, 2, wide, width),
            array(2, 4, rows, width),
            array(2, 4, pair, width),
            array(2, 4, pair, width),
        ],
        in_specs=[
            pl.BlockSpec(memory_space=pl.ANY),
            pl.BlockSpec(memory_space=pltpu.SMEM),
        ]
        + [pl.BlockSpec(memory_space=pl.ANY)] * 4,
        out_specs=[pl.BlockSpec(memory_space=pl.ANY)] * 13,
        scratch_shapes=[
            pltpu.VMEM((CHUNKS, 4, rows, half), f32),
            pltpu.VMEM((4, rows, half), f32),
            pltpu.VMEM((4, 2, 2, rows, half), f32),
            pltpu.VMEM((height, width), f32),
            pltpu.VMEM((2 * band, height), f32),
            *twice(2, height, half),
            *twice(4 * wide, height),
            *twice(2 * band, height),
            *twice(2, height, 2 * band),
            *twice(2, width, width),
            *twice(2 * band, width),
            *twice(2 * band, width),
            pltpu.VMEM((2, 2 * band, width), f32),
            pltpu.VMEM((2 * band, height), f32),
            pltpu.VMEM((4 * wide, width), f32),
            pltpu.VMEM((4, rows, width), f32),
            pltpu.VMEM((4, rows, width), f32),
            pltpu.VMEM((4, rows, width), f32),
            pltpu.SemaphoreType.DMA(()),
        ]
        + [pltpu.SemaphoreType.DMA(shape) for shape in sems],
        compiler_params=pltpu.CompilerParams(
            collective_id=0, has_side_effects=True, vmem_limit_bytes=60 << 20
        ),
        cost_estimate=pl.CostEstimate(flops=products, bytes_accessed=height * width * 80, transcendentals=0),
    )(grad, places, left_basis, right_turned, moment_one, moment_two)
    left_product, right_product, update, new_moment_one, new_moment_two = results[:5]
    new_left = beta_two * left_factor + (1.0 - beta_two) * left_product
    new_right = beta_two * right_factor + (1.0 - beta_two) * right_product
    update_dir = jnp.swapaxes(update, 0, 1)
    new_master = master - learn_rate * (update_dir + decay_weight * master)
    return (new_master, update_dir, new_left, new_right, new_moment_one, new_moment_two)


def solution(mesh):
    shards, tensors, sections = (mesh.shape[name] for name in ("shard", "tensor", "section"))

    def run(*operands):
        own = operands[3].shape[0] // shards
        paired = (shards, tensors, sections, own) == (2, 4, 4, 8)
        band = ("tensor", "section")
        placed = (
            P("shard", "tensor", "section", None, None),
            P(band, "shard", None),
            P(),
            P("shard", band, None),
            P("shard", band, None),
            P("shard", band, None),
            P("shard", None, band),
            P("shard", band, None),
            P("shard", band, None),
        )
        results = (placed[1], placed[1], placed[3], placed[4], placed[7], placed[8])
        return jax.shard_map(
            waved if paired else local,
            mesh=mesh,
            in_specs=placed,
            out_specs=results,
            check_vma=False,
        )(*operands)

    return run
```

```python
import jax
import jax.numpy as jnp
from jax import lax
from jax.experimental import pallas as pl
from jax.experimental.pallas import tpu as pltpu
from jax.sharding import PartitionSpec as P

beta_one = 0.95
beta_two = 0.95
epsilon = 1e-08
learn_rate = 0.01
decay_weight = 0.1
step_count = 10


def slot_table(owner_map, shards):
    owners_flat = owner_map.reshape(-1)
    matrices = owners_flat.shape[0]
    per_owner = matrices // shards
    member = (owners_flat[:, None] == jnp.arange(shards, dtype=jnp.int32)[None, :]).astype(
        jnp.int32
    )
    order = jnp.arange(matrices, dtype=jnp.int32)
    earlier = (order[:, None] > order[None, :]).astype(jnp.int32)
    before = jnp.sum(earlier[:, :, None] * member[None, :, :], axis=1)
    rank_in = jnp.sum(before * member, axis=1)
    slot_of = owners_flat * per_owner + rank_in
    places = (slot_of[:, None] == jnp.arange(matrices, dtype=jnp.int32)[None, :]).astype(jnp.int32)
    source = jnp.sum(places * jnp.arange(matrices, dtype=jnp.int32)[:, None], axis=0)
    return (slot_of, source)


def pick(stacked, indices):
    return jnp.stack(
        [
            lax.dynamic_index_in_dim(stacked, indices[i], 0, keepdims=False)
            for i in range(indices.shape[0])
        ]
    )


def local(
    grad_parts,
    master,
    owner_map,
    left_factor,
    right_factor,
    left_basis,
    right_basis,
    moment_one,
    moment_two,
):
    exact_mode = lax.Precision.HIGHEST
    shards = lax.axis_size("shard")
    members = lax.axis_size(("tensor", "section"))
    position = lax.axis_index(("tensor", "section"))
    slot_of, source = slot_table(owner_map, shards)
    height = left_basis.shape[2]
    width = right_basis.shape[1]
    row_block = height // members
    col_block = width // members
    local_part = grad_parts[0, 0, 0]
    row_piece = lax.psum_scatter(local_part, "shard", scatter_dimension=0, tiled=True)
    stacked = lax.all_gather(row_piece[None], ("tensor", "section"), axis=0, tiled=True)
    ordered = pick(stacked, source)
    full_grad = lax.all_to_all(ordered, "shard", split_axis=0, concat_axis=1, tiled=True)
    full_right = lax.all_gather(right_basis, ("tensor", "section"), axis=2, tiled=True)
    grad_band = lax.dynamic_slice_in_dim(full_grad, position * row_block, row_block, 1)
    grad_slab = lax.dynamic_slice_in_dim(full_grad, position * col_block, col_block, 2)
    new_left = beta_two * left_factor + (1.0 - beta_two) * jnp.einsum(
        "orn,ofn->orf", grad_band, full_grad, precision=exact_mode
    )
    new_right = beta_two * right_factor + (1.0 - beta_two) * jnp.einsum(
        "ofc,ofn->ocn", grad_slab, full_grad, precision=exact_mode
    )
    turned = jnp.einsum("orf,ofn->orn", left_basis, full_grad, precision=exact_mode)
    rotated = jnp.einsum("orn,onk->ork", turned, full_right, precision=exact_mode)
    new_moment_one = beta_one * moment_one + (1.0 - beta_one) * rotated
    new_moment_two = beta_two * moment_two + (1.0 - beta_two) * rotated * rotated
    first_fix = 1.0 - beta_one**step_count
    second_fix = 1.0 - beta_two**step_count
    scaled = new_moment_one / first_fix / (jnp.sqrt(new_moment_two / second_fix) + epsilon)
    pulled = jnp.einsum("orn,okn->ork", scaled, full_right, precision=exact_mode)
    update_dir = lax.psum_scatter(
        jnp.einsum("orf,ork->fok", left_basis, pulled, precision=exact_mode),
        ("tensor", "section"),
        scatter_dimension=0,
        tiled=True,
    )
    new_master = master - learn_rate * (update_dir + decay_weight * master)
    return (new_master, update_dir, new_left, new_right, new_moment_one, new_moment_two)


def halves(value):
    high = value.astype(jnp.bfloat16)
    return high, (value - high.astype(jnp.float32)).astype(jnp.bfloat16)


def triple(first, second, contract):
    def one(a, b):
        return lax.dot_general(a, b, (contract, ((), ())), preferred_element_type=jnp.float32)

    (a, a_low), (b, b_low) = first, second
    return one(a, b) + (one(a, b_low) + one(a_low, b))


PLAIN = ((1,), (0,))
TURNED = ((1,), (1,))
CHUNKS = 4


def banded(
    grad,
    source,
    left,
    right,
    old_one,
    old_two,
    left_out,
    right_out,
    update_out,
    one_out,
    two_out,
    cross,
    pieces,
    full_grad,
    left_half,
    right_full,
    turned_in,
    scaled_in,
    update_in,
    crossed,
    piece,
    load,
    load_left,
    g_hi,
    g_lo,
    gq_hi,
    gq_lo,
    l_hi,
    l_lo,
    lt_hi,
    lt_lo,
    r_hi,
    r_lo,
    p_hi,
    p_lo,
    update,
    left_prod,
    right_prod,
    one,
    two,
    scaled,
    local_sem,
    cross_send,
    cross_recv,
    band_send,
    band_recv,
    mirror_send,
    mirror_recv,
    pick_send,
    pick_recv,
    left_send,
    left_recv,
    right_send,
    right_recv,
    relay_send,
    relay_recv,
    turned_send,
    turned_recv,
    scaled_send,
    scaled_recv,
    hop_send,
    hop_recv,
    update_send,
    update_recv,
    final_send,
    final_recv,
):
    mesh_id = pl.DeviceIdType.MESH
    y, b, z = lax.axis_index("shard"), lax.axis_index("tensor"), lax.axis_index("section")
    h, zin = lax.div(z, 2), lax.rem(z, 2)
    core_z = 1 + h
    inner = (z == 1) | (z == 2)
    rows, height = left.shape[1], left.shape[2]
    cols, width = right.shape[1], right.shape[2]
    half = width // 2
    band = 4 * rows
    pair, wide = 2 * rows, 2 * cols
    tile = min(256, half)
    tiles = width // tile
    tall = 384 if height % 384 == 0 else 128

    def within(start, size, unit=8):
        return pl.ds(pl.multiple_of(start, unit), size)

    def copy(src, dst, send, recv, target):
        return pltpu.make_async_remote_copy(
            src_ref=src,
            dst_ref=dst,
            send_sem=send,
            recv_sem=recv,
            device_id=target,
            device_id_type=mesh_id,
        )

    def give(src, dst, send, recv, target):
        here = (target[0] == y) & (target[1] == b) & (target[2] == z)

        @pl.when(here)
        def _():
            pltpu.make_async_copy(src, dst, send).start()

        @pl.when(jnp.logical_not(here))
        def _():
            copy(src, dst, send, recv, target).start()

    def took(ref, sem):
        pltpu.make_async_copy(ref, ref, sem).wait()

    def fetch(src, dst):
        moved = pltpu.make_async_copy(src, dst, local_sem)
        moved.start()
        moved.wait()

    def fetch_all(moves, whole):
        for src, dst in moves:
            pltpu.make_async_copy(src, dst, local_sem).start()
        took(whole, local_sem)

    def loop(count, body):
        def run(i, carry):
            body(i)
            return carry

        lax.fori_loop(0, count, run, 0)

    barrier = pltpu.get_barrier_semaphore()
    for dy in range(2):
        for db in range(4):
            for dz in range(2):
                if dy or db or dz:
                    other = (
                        lax.rem(y + dy, 2),
                        lax.rem(b + db, 4),
                        2 * h + lax.rem(zin + dz, 2),
                    )
                    pl.semaphore_signal(barrier, inc=1, device_id=other, device_id_type=mesh_id)

    @pl.when(inner)
    def _():
        pl.semaphore_signal(barrier, inc=1, device_id=(y, b, 3 - z), device_id_type=mesh_id)
        pl.semaphore_wait(barrier, 16)

    @pl.when(jnp.logical_not(inner))
    def _():
        pl.semaphore_wait(barrier, 15)

    def lanes(side):
        return within(side * half, half, 128)

    for s in range(CHUNKS):
        copy(
            grad.at[:, pl.ds(s * rows, rows), lanes(1 - y)],
            cross.at[s],
            cross_send.at[s],
            cross_recv.at[s],
            (1 - y, b, z),
        ).start()

    def send_right(w):
        for t in range(4):
            give(
                right.at[4 * w + t],
                right_full.at[w, b, h, within(zin * cols, cols)],
                right_send.at[w, t],
                right_recv.at[w],
                (y, t, z),
            )

    def send_left(w):
        for t in range(4):
            give(
                left.at[4 * w + t],
                left_half.at[w, b, within(zin * rows, rows)],
                left_send.at[w, t],
                left_recv.at[w],
                (y, t, z),
            )

    def drain_right(w):
        for t in range(4):
            took(right.at[0], right_send.at[w, t])

    def drain_left(w):
        for t in range(4):
            took(left.at[0], left_send.at[w, t])

    def drain_bands(s):
        for t in range(4):
            took(crossed.at[t], band_send.at[s, t])

    def drain_scaled(w):
        for t in range(4):
            took(scaled.at[t], scaled_send.at[w, t])

    def hop(place, n):
        copy(place, place, hop_send.at[n], hop_recv.at[n], (y, b, core_z)).start()

    def left_part(w):
        return left_half.at[w, :, within(zin * rows, rows)]

    def right_part(w):
        return right_full.at[w, :, h, within(zin * cols, cols)]

    def band_part(s):
        return pieces.at[s, :, h, zin]

    def scaled_part(w):
        return scaled_in.at[w, :, within(zin * rows, rows)]

    def plane_left(w):
        drain_left(w)
        took(left.at[pl.ds(0, 3)], left_recv.at[w])

    def plane_right(w):
        drain_right(w)
        took(right.at[pl.ds(0, 3)], right_recv.at[w])

    def plane_bands(s):
        drain_bands(s)
        took(crossed.at[pl.ds(0, 3)], band_recv.at[s])

    def plane_scaled(w):
        drain_scaled(w)
        took(scaled.at[pl.ds(0, 3)], scaled_recv.at[w])

    def relay_place(w, part):
        v = zin if part == 0 else 1 - zin
        return right_full.at[w, :, h, within(v * cols, cols)]

    def relay_right(w, part):
        place = relay_place(w, part)
        copy(
            place, place, relay_send.at[w, part], relay_recv.at[w, part], (y, b, 3 - z)
        ).start()

    def relay_hop(w):
        took(right_part(w), hop_recv.at[2 + w])
        relay_right(w, 1)

    def sum_ref(s):
        return (one if s < 2 else two).at[:, :, pl.ds(s % 2 * half, half)]

    def sum_stage(s):
        part = sum_ref(s)
        fetch(grad.at[:, pl.ds(s * rows, rows), lanes(y)], part)
        took(cross.at[s], cross_recv.at[s])
        fetch(cross.at[s], crossed)
        part[...] = part[...] + crossed[...]
        for t in range(4):
            give(
                part.at[t],
                pieces.at[s, b, h, zin],
                band_send.at[s, t],
                band_recv.at[s],
                (y, t, z),
            )

    def mirror_stage(s):
        plane_bands(s)
        took(band_part(s), hop_recv.at[6 + s])
        copy(
            pieces.at[s, :, h],
            pieces.at[s, :, h],
            mirror_send.at[s],
            mirror_recv.at[s],
            (y, b, 3 - z),
        ).start()

    def staged(s, o, t, w):
        return update.at[0, s % 2, pl.ds((4 * o + t) * rows, rows), pl.ds(w * half, half)]

    def drain_pick(s):
        for o in range(2):
            for t in range(4):
                for w in range(2):
                    took(staged(s, o, t, w), pick_send.at[s, o, t, w])

    def pick_stage(s):
        took(pieces.at[s, :, 1 - h], mirror_recv.at[s])
        if s == CHUNKS - 1:
            relay_hop(0)
            relay_right(1, 0)
            relay_hop(1)
        fetch(pieces.at[s], piece)
        if s >= 2:
            drain_pick(s - 2)
        for o in range(2):
            for t in range(4):
                for w in range(2):
                    at = 8 * o + 4 * w + t
                    block = staged(s, o, t, w)
                    block[...] = piece[source[0, at], source[1, at], source[2, at]]
                    give(
                        block,
                        full_grad.at[w, 4 * y + b, pl.ds(s * rows, rows)],
                        pick_send.at[s, o, t, w],
                        pick_recv.at[0],
                        (o, t, z),
                    )

    def edge(body):
        pl.when(jnp.logical_not(inner))(body)

    def edge_right(w):
        plane_right(w)
        hop(right_part(w), 2 + w)

    def edge_left(w):
        plane_left(w)
        hop(left_part(w), w)

    def gather_gradients():
        send_right(0)
        for s in range(CHUNKS):
            sum_stage(s)

            @pl.when(jnp.logical_not(inner))
            def _():
                plane_bands(s)
                hop(band_part(s), 6 + s)
                if s == 1:
                    edge_right(0)
                if s == 3:
                    edge_left(0)

            if s == 0:
                send_left(0)
            if s == 1:
                send_right(1)
            if s == 2:
                send_left(1)

            @pl.when(inner)
            def _():
                if s == 0:
                    plane_right(0)
                    relay_right(0, 0)
                if s == 3:
                    plane_right(1)
                if s >= 1:
                    mirror_stage(s - 1)
                if s >= 2:
                    pick_stage(s - 2)

    def prepare(w):
        fetch_all(
            [
                (
                    full_grad.at[w, 4 * side + t],
                    load.at[pl.ds(t * band, band), pl.ds(side * half, half)],
                )
                for side in range(2)
                for t in range(4)
            ],
            full_grad.at[w],
        )

        def by_rows(i):
            at = within(i * pair, pair, 16)
            high, low = halves(load[at, :])
            for side in range(2):
                g_hi[side, at, :] = high[:, side * half : (side + 1) * half]
                g_lo[side, at, :] = low[:, side * half : (side + 1) * half]

        loop(8, by_rows)

        def by_columns(t):
            own = load[pl.ds(0, height), within((2 * t + h) * wide, wide, wide)]
            high, low = halves(own.T)
            at = within(t * wide, wide, 16)
            gq_hi[at, pl.ds(0, height)] = high
            gq_lo[at, pl.ds(0, height)] = low

        loop(4, by_columns)

    def prepare_left(w):
        plane_left(w)
        took(left_part(w), hop_recv.at[w])
        fetch_all(
            [(left_half.at[w, t], load_left.at[pl.ds(t * pair, pair)]) for t in range(4)],
            left_half.at[w],
        )

        def by_rows(t):
            at = within(t * pair, pair, 16)
            high, low = halves(load_left[at, :])
            l_hi[at, :] = high
            l_lo[at, :] = low

        loop(4, by_rows)

        def by_columns(i):
            at = within(i * 128, 128, 128)
            high, low = halves(load_left[:, at].T)
            lt_hi[w, at, :] = high
            lt_lo[w, at, :] = low

        loop(height // 128, by_columns)

    def prepare_right(w):
        for part in range(2):
            took(relay_place(w, part), relay_recv.at[w, part])
        fetch_all(
            [
                (right_full.at[w, t, v], load.at[pl.ds((2 * t + v) * wide, wide)])
                for t in range(4)
                for v in range(2)
            ],
            right_full.at[w],
        )

        def by_rows(i):
            at = within(i * wide, wide, 16)
            high, low = halves(load[at, :])
            r_hi[w, at, :] = high
            r_lo[w, at, :] = low

        loop(8, by_rows)

    def turn(w):
        for m in range(2):
            at = pl.ds(m * band, band)

            def body(n):
                side, spot = n // (tiles // 2), within(n % (tiles // 2) * tile, tile, tile)
                product = triple(
                    (l_hi[at, :], l_lo[at, :]),
                    (g_hi[side, :, spot], g_lo[side, :, spot]),
                    PLAIN,
                )
                high, low = halves(product)
                into = within(n * tile, tile, tile)
                p_hi[at, into] = high
                p_lo[at, into] = low

            loop(tiles, body)

    def rotated(t, v):
        return load_left.at[pl.ds(t * pair + v * rows, rows), pl.ds(0, width)]

    def drain_turned(w):
        for t in range(4):
            for v in range(2):
                took(rotated(t, v), turned_send.at[w, t, v])

    def rotate(w):
        for m in range(2):
            at = pl.ds(m * band, band)

            def body(n):
                spot = within(n * tile, tile, tile)
                load_left[at, spot] = triple(
                    (p_hi[at, :], p_lo[at, :]), (r_hi[w, spot, :], r_lo[w, spot, :]), TURNED
                )

            loop(tiles, body)
            for t in (2 * m, 2 * m + 1):
                for v in range(2):
                    give(
                        rotated(t, v),
                        turned_in.at[w, b],
                        turned_send.at[w, t, v],
                        turned_recv.at[w],
                        (y, t, 2 * h + v),
                    )

    def drain_left_product(w):
        for t in range(4):
            for v in range(2):
                took(left_prod.at[w, pl.ds(0, rows)], final_send.at[0, w, t, v])

    def drain_right_product(w):
        for t in range(4):
            for v in range(2):
                took(right_prod.at[w, pl.ds(0, cols)], final_send.at[1, w, t, v])

    def left_product(w):
        for m in range(2):
            at = pl.ds(m * band, band)
            spots = [within(t * band + h * pair, pair, 16) for t in (2 * m, 2 * m + 1)]

            def body(n):
                spot = within(n * tall, tall, 128)
                total = None
                for side in range(2):
                    own = [
                        jnp.concatenate([g[side, one_spot, :] for one_spot in spots], axis=0)
                        for g in (g_hi, g_lo)
                    ]
                    product = triple(own, (g_hi[side, spot, :], g_lo[side, spot, :]), TURNED)
                    total = product if total is None else total + product
                left_prod[w, at, spot] = total

            loop(height // tall, body)

    def send_left_product(w):
        for t in range(4):
            for v in range(2):
                give(
                    left_prod.at[w, pl.ds(t * pair + v * rows, rows)],
                    left_out.at[4 * w + b],
                    final_send.at[0, w, t, v],
                    final_recv.at[0],
                    (y, t, 2 * h + v),
                )

    def right_product(w):
        for m in range(2):
            at = pl.ds(m * 2 * wide, 2 * wide)

            def body(n):
                side, spot = n // (tiles // 2), within(n % (tiles // 2) * tile, tile, tile)
                right_prod[w, at, within(n * tile, tile, tile)] = triple(
                    (gq_hi[at, pl.ds(0, height)], gq_lo[at, pl.ds(0, height)]),
                    (g_hi[side, :, spot], g_lo[side, :, spot]),
                    PLAIN,
                )

            loop(tiles, body)

    def send_right_product(w):
        for t in range(4):
            for v in range(2):
                give(
                    right_prod.at[w, pl.ds(t * wide + v * cols, cols)],
                    right_out.at[4 * w + b],
                    final_send.at[1, w, t, v],
                    final_recv.at[1],
                    (y, t, 2 * h + v),
                )

    def moments(w):
        slots = pl.ds(4 * w, 4)
        fetch_all([(old_one.at[slots], one)], one)
        fetch_all([(old_two.at[slots], two)], two)

        @pl.when(inner)
        def _():
            if w:
                drain_turned(w)
            took(old_one.at[pl.ds(0, 3)], turned_recv.at[w])

        @pl.when(jnp.logical_not(inner))
        def _():
            took(old_one.at[pl.ds(0, 4)], turned_recv.at[w])

        fetch(turned_in.at[w], scaled)
        first_fix = 1.0 - beta_one**step_count
        second_fix = 1.0 - beta_two**step_count
        for t in range(4):

            def body(i):
                at = within(i * 8, 8)
                value = scaled[t, at, :]
                new_one = beta_one * one[t, at, :] + (1.0 - beta_one) * value
                new_two = beta_two * two[t, at, :] + (1.0 - beta_two) * value * value
                one[t, at, :] = new_one
                two[t, at, :] = new_two
                scaled[t, at, :] = (
                    new_one / first_fix / (jnp.sqrt(new_two / second_fix) + epsilon)
                )

            loop(rows // 8, body)
            give(
                scaled.at[t],
                scaled_in.at[w, b, within(zin * rows, rows)],
                scaled_send.at[w, t],
                scaled_recv.at[w],
                (y, t, z),
            )

        @pl.when(jnp.logical_not(inner))
        def _():
            plane_scaled(w)
            hop(scaled_part(w), 4 + w)

        fetch(one, one_out.at[slots])
        fetch(two, two_out.at[slots])

    def pull(w):
        plane_scaled(w)
        took(scaled_part(w), hop_recv.at[4 + w])
        fetch_all(
            [(scaled_in.at[w, t], load.at[pl.ds(t * pair, pair)]) for t in range(4)],
            scaled_in.at[w],
        )

        def by_rows(t):
            at = within(t * pair, pair, 16)
            high, low = halves(load[at, :])
            p_hi[at, :] = high
            p_lo[at, :] = low

        loop(4, by_rows)
        for m in range(2):
            at = pl.ds(m * band, band)

            def body(n):
                spot = within(n * tile, tile, tile)
                high, low = halves(
                    triple((p_hi[at, :], p_lo[at, :]), (r_hi[w, :, spot], r_lo[w, :, spot]), PLAIN)
                )
                gq_hi[at, spot] = high
                gq_lo[at, spot] = low

            loop(tiles, body)

    def mirrored(w, t):
        return update.at[w, 0, pl.ds(t * pair, pair)]

    def drain_update(w):
        for t in range(4):
            took(mirrored(w, t), update_send.at[w, t])
            for v in range(2):
                took(update.at[w, 1, pl.ds(0, rows)], final_send.at[2, w, t, v])

    def back(w):
        own_rows = pl.ds(0, 2 * band)
        for slot, side in ((0, 1 - h), (1, h)):
            for m in range(2):
                at = pl.ds(m * band, band)
                spots = [within(t * band + side * pair, pair, 16) for t in (2 * m, 2 * m + 1)]

                def body(n):
                    spot = within(n * tile, tile, tile)
                    own = [
                        jnp.concatenate([turned[w, one_spot, :] for one_spot in spots], axis=0)
                        for turned in (lt_hi, lt_lo)
                    ]
                    update[w, slot, at, spot] = triple(own, (gq_hi[own_rows, spot], gq_lo[own_rows, spot]), PLAIN)

                loop(tiles, body)
                if slot == 0:
                    for t in (2 * m, 2 * m + 1):
                        copy(
                            mirrored(w, t),
                            update_in.at[w, t],
                            update_send.at[w, t],
                            update_recv.at[w, t],
                            (y, b, 3 - z),
                        ).start()

    def finish(w):
        for t in range(4):
            took(update_in.at[w, t], update_recv.at[w, t])
            at = pl.ds(t * pair, pair)
            fetch(update_in.at[w, t], load.at[at])
            update[w, 1, at] = update[w, 1, at] + load[at, :]
            for v in range(2):
                give(
                    update.at[w, 1, pl.ds(t * pair + v * rows, rows)],
                    update_out.at[4 * w + b],
                    final_send.at[2, w, t, v],
                    final_recv.at[2],
                    (y, t, 2 * h + v),
                )

    gather_gradients()

    @pl.when(inner)
    def _():
        mirror_stage(CHUNKS - 1)
        for s in (CHUNKS - 2, CHUNKS - 1):
            pick_stage(s)
        for s in (CHUNKS - 2, CHUNKS - 1):
            drain_pick(s)
        took(full_grad.at[:, pl.ds(0, 7)], pick_recv.at[0])
        prepare(0)
        prepare_left(0)
        turn(0)
        prepare_right(0)
        rotate(0)
        right_product(0)
        left_product(0)
        prepare(1)
        drain_turned(0)
        send_right_product(0)
        prepare_left(1)
        turn(1)

    @pl.when(jnp.logical_not(inner))
    def _():
        edge_right(1)
        edge_left(1)

    moments(0)

    @pl.when(inner)
    def _():
        prepare_right(1)
        rotate(1)
        send_left_product(0)
        right_product(1)
        left_product(1)
        pull(0)
        back(0)

    moments(1)

    @pl.when(inner)
    def _():
        send_right_product(1)
        send_left_product(1)
        pull(1)
        back(1)
        finish(0)
        finish(1)
        drain_left_product(0)
        drain_right_product(0)
        drain_left_product(1)
        drain_right_product(1)
        drain_update(0)
        drain_update(1)
        for s in range(CHUNKS):
            took(pieces.at[s, :, h], mirror_send.at[s])
        for w in range(2):
            for part in range(2):
                took(relay_place(w, part), relay_send.at[w, part])
        took(left.at[pl.ds(0, 6)], final_recv.at[0])
        took(right.at[pl.ds(0, 6)], final_recv.at[1])
        took(old_one.at[pl.ds(0, 6)], final_recv.at[2])

    @pl.when(jnp.logical_not(inner))
    def _():
        for w in range(2):
            took(left_part(w), hop_send.at[w])
            took(right_part(w), hop_send.at[2 + w])
            took(scaled_part(w), hop_send.at[4 + w])
        for s in range(CHUNKS):
            took(band_part(s), hop_send.at[6 + s])
        took(left, final_recv.at[0])
        took(right, final_recv.at[1])
        took(old_one, final_recv.at[2])

    for s in range(CHUNKS):
        took(cross.at[s], cross_send.at[s])


def waved(
    grad_parts,
    master,
    owner_map,
    left_factor,
    right_factor,
    left_basis,
    right_basis,
    moment_one,
    moment_two,
):
    _, source = slot_table(owner_map, lax.axis_size("shard"))
    places = jnp.stack((source // 4, source % 4 // 2, source % 2))
    slots, rows, height = left_basis.shape
    width = right_basis.shape[1]
    cols, half, band, pair, wide = width // 16, width // 2, 4 * rows, 2 * rows, width // 8
    f32, bf16 = jnp.float32, jnp.bfloat16
    right_turned = jnp.swapaxes(right_basis, 1, 2)
    grad = grad_parts[0, 0, 0].reshape(4, band, width)

    def array(*shape):
        return jax.ShapeDtypeStruct(shape, f32)

    def twice(*shape):
        return [pltpu.VMEM(shape, bf16)] * 2

    sems = [
        (CHUNKS,),
        (CHUNKS,),
        (CHUNKS, 4),
        (CHUNKS,),
        (CHUNKS,),
        (CHUNKS,),
        (CHUNKS, 2, 4, 2),
        (1,),
        (2, 4),
        (2,),
        (2, 4),
        (2,),
        (2, 2),
        (2, 2),
        (2, 4, 2),
        (2,),
        (2, 4),
        (2,),
        (6 + CHUNKS,),
        (6 + CHUNKS,),
        (2, 4),
        (2, 4),
        (3, 2, 4, 2),
        (3,),
    ]
    products = 6 * 2 * 2 * height * height * width
    results = pl.pallas_call(
        banded,
        out_shape=[
            array(slots, rows, height),
            array(slots, cols, width),
            array(slots, rows, width),
            array(slots, rows, width),
            array(slots, rows, width),
            array(CHUNKS, 4, rows, half),
            array(CHUNKS, 4, 2, 2, rows, half),
            array(2, 8, band, half),
            array(2, 4, pair, height),
            array(2, 4, 2, wide, width),
            array(2, 4, rows, width),
            array(2, 4, pair, width),
            array(2, 4, pair, width),
        ],
        in_specs=[
            pl.BlockSpec(memory_space=pl.ANY),
            pl.BlockSpec(memory_space=pltpu.SMEM),
        ]
        + [pl.BlockSpec(memory_space=pl.ANY)] * 4,
        out_specs=[pl.BlockSpec(memory_space=pl.ANY)] * 13,
        scratch_shapes=[
            pltpu.VMEM((4, rows, half), f32),
            pltpu.VMEM((4, 2, 2, rows, half), f32),
            pltpu.VMEM((height, width), f32),
            pltpu.VMEM((2 * band, height), f32),
            *twice(2, height, half),
            *twice(max(4 * wide, 2 * band), max(height, width)),
            *twice(2 * band, height),
            *twice(2, height, 2 * band),
            *twice(2, width, width),
            *twice(2 * band, width),
            pltpu.VMEM((2, 2, 2 * band, width), f32),
            pltpu.VMEM((2, 2 * band, height), f32),
            pltpu.VMEM((2, 4 * wide, width), f32),
            pltpu.VMEM((4, rows, width), f32),
            pltpu.VMEM((4, rows, width), f32),
            pltpu.VMEM((4, rows, width), f32),
            pltpu.SemaphoreType.DMA(()),
        ]
        + [pltpu.SemaphoreType.DMA(shape) for shape in sems],
        compiler_params=pltpu.CompilerParams(
            collective_id=0, has_side_effects=True, vmem_limit_bytes=60 << 20
        ),
        cost_estimate=pl.CostEstimate(flops=products, bytes_accessed=height * width * 80, transcendentals=0),
    )(grad, places, left_basis, right_turned, moment_one, moment_two)
    left_product, right_product, update, new_moment_one, new_moment_two = results[:5]
    new_left = beta_two * left_factor + (1.0 - beta_two) * left_product
    new_right = beta_two * right_factor + (1.0 - beta_two) * right_product
    update_dir = jnp.swapaxes(update, 0, 1)
    new_master = master - learn_rate * (update_dir + decay_weight * master)
    return (new_master, update_dir, new_left, new_right, new_moment_one, new_moment_two)


def solution(mesh):
    shards, tensors, sections = (mesh.shape[name] for name in ("shard", "tensor", "section"))

    def run(*operands):
        own = operands[3].shape[0] // shards
        paired = (shards, tensors, sections, own) == (2, 4, 4, 8)
        band = ("tensor", "section")
        placed = (
            P("shard", "tensor", "section", None, None),
            P(band, "shard", None),
            P(),
            P("shard", band, None),
            P("shard", band, None),
            P("shard", band, None),
            P("shard", None, band),
            P("shard", band, None),
            P("shard", band, None),
        )
        results = (placed[1], placed[1], placed[3], placed[4], placed[7], placed[8])
        return jax.shard_map(
            waved if paired else local,
            mesh=mesh,
            in_specs=placed,
            out_specs=results,
            check_vma=False,
        )(*operands)

    return run
```

```python
import jax
import jax.numpy as jnp
from jax import lax
from jax.experimental import pallas as pl
from jax.experimental.pallas import tpu as pltpu
from jax.sharding import PartitionSpec as P

beta_one = 0.95
beta_two = 0.95
epsilon = 1e-08
learn_rate = 0.01
decay_weight = 0.1
step_count = 10


def slot_table(owner_map, shards):
    owners_flat = owner_map.reshape(-1)
    matrices = owners_flat.shape[0]
    per_owner = matrices // shards
    member = (owners_flat[:, None] == jnp.arange(shards, dtype=jnp.int32)[None, :]).astype(
        jnp.int32
    )
    order = jnp.arange(matrices, dtype=jnp.int32)
    earlier = (order[:, None] > order[None, :]).astype(jnp.int32)
    before = jnp.sum(earlier[:, :, None] * member[None, :, :], axis=1)
    rank_in = jnp.sum(before * member, axis=1)
    slot_of = owners_flat * per_owner + rank_in
    places = (slot_of[:, None] == jnp.arange(matrices, dtype=jnp.int32)[None, :]).astype(jnp.int32)
    source = jnp.sum(places * jnp.arange(matrices, dtype=jnp.int32)[:, None], axis=0)
    return (slot_of, source)


def pick(stacked, indices):
    return jnp.stack(
        [
            lax.dynamic_index_in_dim(stacked, indices[i], 0, keepdims=False)
            for i in range(indices.shape[0])
        ]
    )


def local(
    grad_parts,
    master,
    owner_map,
    left_factor,
    right_factor,
    left_basis,
    right_basis,
    moment_one,
    moment_two,
):
    exact_mode = lax.Precision.HIGHEST
    shards = lax.axis_size("shard")
    members = lax.axis_size(("tensor", "section"))
    position = lax.axis_index(("tensor", "section"))
    slot_of, source = slot_table(owner_map, shards)
    height = left_basis.shape[2]
    width = right_basis.shape[1]
    row_block = height // members
    col_block = width // members
    local_part = grad_parts[0, 0, 0]
    row_piece = lax.psum_scatter(local_part, "shard", scatter_dimension=0, tiled=True)
    stacked = lax.all_gather(row_piece[None], ("tensor", "section"), axis=0, tiled=True)
    ordered = pick(stacked, source)
    full_grad = lax.all_to_all(ordered, "shard", split_axis=0, concat_axis=1, tiled=True)
    full_right = lax.all_gather(right_basis, ("tensor", "section"), axis=2, tiled=True)
    grad_band = lax.dynamic_slice_in_dim(full_grad, position * row_block, row_block, 1)
    grad_slab = lax.dynamic_slice_in_dim(full_grad, position * col_block, col_block, 2)
    new_left = beta_two * left_factor + (1.0 - beta_two) * jnp.einsum(
        "orn,ofn->orf", grad_band, full_grad, precision=exact_mode
    )
    new_right = beta_two * right_factor + (1.0 - beta_two) * jnp.einsum(
        "ofc,ofn->ocn", grad_slab, full_grad, precision=exact_mode
    )
    turned = jnp.einsum("orf,ofn->orn", left_basis, full_grad, precision=exact_mode)
    rotated = jnp.einsum("orn,onk->ork", turned, full_right, precision=exact_mode)
    new_moment_one = beta_one * moment_one + (1.0 - beta_one) * rotated
    new_moment_two = beta_two * moment_two + (1.0 - beta_two) * rotated * rotated
    first_fix = 1.0 - beta_one**step_count
    second_fix = 1.0 - beta_two**step_count
    scaled = new_moment_one / first_fix / (jnp.sqrt(new_moment_two / second_fix) + epsilon)
    pulled = jnp.einsum("orn,okn->ork", scaled, full_right, precision=exact_mode)
    update_dir = lax.psum_scatter(
        jnp.einsum("orf,ork->fok", left_basis, pulled, precision=exact_mode),
        ("tensor", "section"),
        scatter_dimension=0,
        tiled=True,
    )
    new_master = master - learn_rate * (update_dir + decay_weight * master)
    return (new_master, update_dir, new_left, new_right, new_moment_one, new_moment_two)


def halves(value):
    high = value.astype(jnp.bfloat16)
    return high, (value - high.astype(jnp.float32)).astype(jnp.bfloat16)


def triple(first, second, contract):
    def one(a, b):
        return lax.dot_general(a, b, (contract, ((), ())), preferred_element_type=jnp.float32)

    (a, a_low), (b, b_low) = first, second
    return one(a, b) + (one(a, b_low) + one(a_low, b))


PLAIN = ((1,), (0,))
TURNED = ((1,), (1,))
CHUNKS = 6


def banded(
    grad,
    source,
    left,
    right,
    old_one,
    old_two,
    left_out,
    right_out,
    update_out,
    one_out,
    two_out,
    cross,
    pieces,
    full_grad,
    left_half,
    right_full,
    turned_in,
    scaled_in,
    update_in,
    crossed,
    piece,
    load,
    load_left,
    g_hi,
    g_lo,
    gq_hi,
    gq_lo,
    l_hi,
    l_lo,
    lt_hi,
    lt_lo,
    r_hi,
    r_lo,
    p_hi,
    p_lo,
    update,
    left_prod,
    right_prod,
    one,
    two,
    scaled,
    local_sem,
    cross_send,
    cross_recv,
    band_send,
    band_recv,
    mirror_send,
    mirror_recv,
    pick_send,
    pick_recv,
    left_send,
    left_recv,
    right_send,
    right_recv,
    relay_send,
    relay_recv,
    turned_send,
    turned_recv,
    scaled_send,
    scaled_recv,
    hop_send,
    hop_recv,
    update_send,
    update_recv,
    final_send,
    final_recv,
):
    mesh_id = pl.DeviceIdType.MESH
    y, b, z = lax.axis_index("shard"), lax.axis_index("tensor"), lax.axis_index("section")
    h, zin = lax.div(z, 2), lax.rem(z, 2)
    core_z = 1 + h
    inner = (z == 1) | (z == 2)
    rows, height = left.shape[1], left.shape[2]
    cols, width = right.shape[1], right.shape[2]
    half = width // 2
    band = 4 * rows
    step = band // CHUNKS
    pair, wide = 2 * rows, 2 * cols
    tile = min(256, half)
    tiles = width // tile
    tall = 384 if height % 384 == 0 else 128

    def within(start, size, unit=8):
        return pl.ds(pl.multiple_of(start, unit), size)

    def copy(src, dst, send, recv, target):
        return pltpu.make_async_remote_copy(
            src_ref=src,
            dst_ref=dst,
            send_sem=send,
            recv_sem=recv,
            device_id=target,
            device_id_type=mesh_id,
        )

    def give(src, dst, send, recv, target):
        here = (target[0] == y) & (target[1] == b) & (target[2] == z)

        @pl.when(here)
        def _():
            pltpu.make_async_copy(src, dst, send).start()

        @pl.when(jnp.logical_not(here))
        def _():
            copy(src, dst, send, recv, target).start()

    def took(ref, sem):
        pltpu.make_async_copy(ref, ref, sem).wait()

    def fetch(src, dst):
        moved = pltpu.make_async_copy(src, dst, local_sem)
        moved.start()
        moved.wait()

    def fetch_all(moves, whole):
        for src, dst in moves:
            pltpu.make_async_copy(src, dst, local_sem).start()
        took(whole, local_sem)

    def loop(count, body):
        def run(i, carry):
            body(i)
            return carry

        lax.fori_loop(0, count, run, 0)

    barrier = pltpu.get_barrier_semaphore()
    for dy in range(2):
        for db in range(4):
            for dz in range(2):
                if dy or db or dz:
                    other = (
                        lax.rem(y + dy, 2),
                        lax.rem(b + db, 4),
                        2 * h + lax.rem(zin + dz, 2),
                    )
                    pl.semaphore_signal(barrier, inc=1, device_id=other, device_id_type=mesh_id)

    @pl.when(inner)
    def _():
        pl.semaphore_signal(barrier, inc=1, device_id=(y, b, 3 - z), device_id_type=mesh_id)
        pl.semaphore_wait(barrier, 16)

    @pl.when(jnp.logical_not(inner))
    def _():
        pl.semaphore_wait(barrier, 15)

    def lanes(side):
        return within(side * half, half, 128)

    for s in range(CHUNKS):
        copy(
            grad.at[:, pl.ds(s * step, step), lanes(1 - y)],
            cross.at[s],
            cross_send.at[s],
            cross_recv.at[s],
            (1 - y, b, z),
        ).start()

    def send_right(w):
        for t in range(4):
            give(
                right.at[4 * w + t],
                right_full.at[w, b, h, within(zin * cols, cols)],
                right_send.at[w, t],
                right_recv.at[w],
                (y, t, z),
            )

    def send_left(w):
        for t in range(4):
            give(
                left.at[4 * w + t],
                left_half.at[w, b, within(zin * rows, rows)],
                left_send.at[w, t],
                left_recv.at[w],
                (y, t, z),
            )

    def drain_right(w):
        for t in range(4):
            took(right.at[0], right_send.at[w, t])

    def drain_left(w):
        for t in range(4):
            took(left.at[0], left_send.at[w, t])

    def drain_bands(s):
        for t in range(4):
            took(crossed.at[t], band_send.at[s, t])

    def drain_scaled(w):
        for t in range(4):
            took(scaled.at[t], scaled_send.at[w, t])

    def hop(place, n):
        copy(place, place, hop_send.at[n], hop_recv.at[n], (y, b, core_z)).start()

    def left_part(w):
        return left_half.at[w, :, within(zin * rows, rows)]

    def right_part(w):
        return right_full.at[w, :, h, within(zin * cols, cols)]

    def band_part(s):
        return pieces.at[s, :, h, zin]

    def scaled_part(w):
        return scaled_in.at[w, :, within(zin * rows, rows)]

    def plane_left(w):
        drain_left(w)
        took(left.at[pl.ds(0, 3)], left_recv.at[w])

    def plane_right(w):
        drain_right(w)
        took(right.at[pl.ds(0, 3)], right_recv.at[w])

    def plane_bands(s):
        drain_bands(s)
        took(crossed.at[pl.ds(0, 3)], band_recv.at[s])

    def plane_scaled(w):
        drain_scaled(w)
        took(scaled.at[pl.ds(0, 3)], scaled_recv.at[w])

    def relay_place(w, part):
        v = zin if part == 0 else 1 - zin
        return right_full.at[w, :, h, within(v * cols, cols)]

    def relay_right(w, part):
        place = relay_place(w, part)
        copy(
            place, place, relay_send.at[w, part], relay_recv.at[w, part], (y, b, 3 - z)
        ).start()

    def relay_hop(w):
        took(right_part(w), hop_recv.at[2 + w])
        relay_right(w, 1)

    def sum_ref(s):
        holder = (one, two, scaled)[s // 2 % 3]
        return holder.at[:, pl.ds(0, step), pl.ds(s % 2 * half, half)]

    def sum_stage(s):
        part = sum_ref(s)
        fetch(grad.at[:, pl.ds(s * step, step), lanes(y)], part)
        took(cross.at[s], cross_recv.at[s])
        fetch(cross.at[s], crossed)
        part[...] = part[...] + crossed[...]
        for t in range(4):
            give(
                part.at[t],
                pieces.at[s, b, h, zin],
                band_send.at[s, t],
                band_recv.at[s],
                (y, t, z),
            )

    def mirror_stage(s):
        plane_bands(s)
        took(band_part(s), hop_recv.at[6 + s])
        copy(
            pieces.at[s, :, h],
            pieces.at[s, :, h],
            mirror_send.at[s],
            mirror_recv.at[s],
            (y, b, 3 - z),
        ).start()

    def staged(s, o, t, w):
        return update.at[0, s % 2, pl.ds((4 * o + t) * step, step), pl.ds(w * half, half)]

    def drain_pick(s):
        for o in range(2):
            for t in range(4):
                for w in range(2):
                    took(staged(s, o, t, w), pick_send.at[s % 2, o, t, w])

    def pick_stage(s):
        took(pieces.at[s, :, 1 - h], mirror_recv.at[s])
        if s == CHUNKS - 1:
            relay_hop(0)
            relay_right(1, 0)
            relay_hop(1)
        fetch(pieces.at[s], piece)
        if s >= 2:
            drain_pick(s - 2)
        for o in range(2):
            for t in range(4):
                for w in range(2):
                    at = 8 * o + 4 * w + t
                    block = staged(s, o, t, w)
                    block[...] = piece[source[0, at], source[1, at], source[2, at]]
                    give(
                        block,
                        full_grad.at[w, 4 * y + b, pl.ds(s * step, step)],
                        pick_send.at[s % 2, o, t, w],
                        pick_recv.at[0],
                        (o, t, z),
                    )

    def edge(body):
        pl.when(jnp.logical_not(inner))(body)

    def edge_right(w):
        plane_right(w)
        hop(right_part(w), 2 + w)

    def edge_left(w):
        plane_left(w)
        hop(left_part(w), w)

    def gather_gradients():
        send_right(0)
        for s in range(CHUNKS):
            sum_stage(s)

            @pl.when(jnp.logical_not(inner))
            def _():
                plane_bands(s)
                hop(band_part(s), 6 + s)
                if s == 1:
                    edge_right(0)
                if s == 3:
                    edge_left(0)

            if s == 0:
                send_left(0)
            if s == 1:
                send_right(1)
            if s == 2:
                send_left(1)

            @pl.when(inner)
            def _():
                if s == 0:
                    plane_right(0)
                    relay_right(0, 0)
                if s == 4:
                    plane_right(1)
                if s >= 1:
                    mirror_stage(s - 1)
                if s >= 2:
                    pick_stage(s - 2)

    def prepare(w):
        fetch_all(
            [
                (
                    full_grad.at[w, 4 * side + t],
                    load.at[pl.ds(t * band, band), pl.ds(side * half, half)],
                )
                for side in range(2)
                for t in range(4)
            ],
            full_grad.at[w],
        )

        def by_rows(i):
            at = within(i * pair, pair, 16)
            high, low = halves(load[at, :])
            for side in range(2):
                g_hi[side, at, :] = high[:, side * half : (side + 1) * half]
                g_lo[side, at, :] = low[:, side * half : (side + 1) * half]

        loop(8, by_rows)

        def by_columns(t):
            own = load[pl.ds(0, height), within((2 * t + h) * wide, wide, wide)]
            high, low = halves(own.T)
            at = within(t * wide, wide, 16)
            gq_hi[at, pl.ds(0, height)] = high
            gq_lo[at, pl.ds(0, height)] = low

        loop(4, by_columns)

    def prepare_left(w):
        plane_left(w)
        took(left_part(w), hop_recv.at[w])
        fetch_all(
            [(left_half.at[w, t], load_left.at[pl.ds(t * pair, pair)]) for t in range(4)],
            left_half.at[w],
        )

        def by_rows(t):
            at = within(t * pair, pair, 16)
            high, low = halves(load_left[at, :])
            l_hi[at, :] = high
            l_lo[at, :] = low

        loop(4, by_rows)

        def by_columns(i):
            at = within(i * 128, 128, 128)
            high, low = halves(load_left[:, at].T)
            lt_hi[w, at, :] = high
            lt_lo[w, at, :] = low

        loop(height // 128, by_columns)

    def prepare_right(w):
        for part in range(2):
            took(relay_place(w, part), relay_recv.at[w, part])
        fetch_all(
            [
                (right_full.at[w, t, v], load.at[pl.ds((2 * t + v) * wide, wide)])
                for t in range(4)
                for v in range(2)
            ],
            right_full.at[w],
        )

        def by_rows(i):
            at = within(i * wide, wide, 16)
            high, low = halves(load[at, :])
            r_hi[w, at, :] = high
            r_lo[w, at, :] = low

        loop(8, by_rows)

    def turn(w):
        for m in range(2):
            at = pl.ds(m * band, band)

            def body(n):
                side, spot = n // (tiles // 2), within(n % (tiles // 2) * tile, tile, tile)
                product = triple(
                    (l_hi[at, :], l_lo[at, :]),
                    (g_hi[side, :, spot], g_lo[side, :, spot]),
                    PLAIN,
                )
                high, low = halves(product)
                into = within(n * tile, tile, tile)
                p_hi[at, into] = high
                p_lo[at, into] = low

            loop(tiles, body)

    def rotated(t, v):
        return load_left.at[pl.ds(t * pair + v * rows, rows), pl.ds(0, width)]

    def drain_turned(w):
        for t in range(4):
            for v in range(2):
                took(rotated(t, v), turned_send.at[w, t, v])

    def rotate(w):
        for m in range(2):
            at = pl.ds(m * band, band)

            def body(n):
                spot = within(n * tile, tile, tile)
                load_left[at, spot] = triple(
                    (p_hi[at, :], p_lo[at, :]), (r_hi[w, spot, :], r_lo[w, spot, :]), TURNED
                )

            loop(tiles, body)
            for t in (2 * m, 2 * m + 1):
                for v in range(2):
                    give(
                        rotated(t, v),
                        turned_in.at[w, b],
                        turned_send.at[w, t, v],
                        turned_recv.at[w],
                        (y, t, 2 * h + v),
                    )

    def drain_left_product(w):
        for t in range(4):
            for v in range(2):
                took(left_prod.at[w, pl.ds(0, rows)], final_send.at[0, w, t, v])

    def drain_right_product(w):
        for t in range(4):
            for v in range(2):
                took(right_prod.at[w, pl.ds(0, cols)], final_send.at[1, w, t, v])

    def left_product(w):
        for m in range(2):
            at = pl.ds(m * band, band)
            spots = [within(t * band + h * pair, pair, 16) for t in (2 * m, 2 * m + 1)]

            def body(n):
                spot = within(n * tall, tall, 128)
                total = None
                for side in range(2):
                    own = [
                        jnp.concatenate([g[side, one_spot, :] for one_spot in spots], axis=0)
                        for g in (g_hi, g_lo)
                    ]
                    product = triple(own, (g_hi[side, spot, :], g_lo[side, spot, :]), TURNED)
                    total = product if total is None else total + product
                left_prod[w, at, spot] = total

            loop(height // tall, body)

    def send_left_product(w):
        for t in range(4):
            for v in range(2):
                give(
                    left_prod.at[w, pl.ds(t * pair + v * rows, rows)],
                    left_out.at[4 * w + b],
                    final_send.at[0, w, t, v],
                    final_recv.at[0],
                    (y, t, 2 * h + v),
                )

    def right_product(w):
        for m in range(2):
            at = pl.ds(m * 2 * wide, 2 * wide)

            def body(n):
                side, spot = n // (tiles // 2), within(n % (tiles // 2) * tile, tile, tile)
                right_prod[w, at, within(n * tile, tile, tile)] = triple(
                    (gq_hi[at, pl.ds(0, height)], gq_lo[at, pl.ds(0, height)]),
                    (g_hi[side, :, spot], g_lo[side, :, spot]),
                    PLAIN,
                )

            loop(tiles, body)

    def send_right_product(w):
        for t in range(4):
            for v in range(2):
                give(
                    right_prod.at[w, pl.ds(t * wide + v * cols, cols)],
                    right_out.at[4 * w + b],
                    final_send.at[1, w, t, v],
                    final_recv.at[1],
                    (y, t, 2 * h + v),
                )

    def moments(w):
        slots = pl.ds(4 * w, 4)
        fetch_all([(old_one.at[slots], one)], one)
        fetch_all([(old_two.at[slots], two)], two)

        @pl.when(inner)
        def _():
            if w:
                drain_turned(w)
            took(old_one.at[pl.ds(0, 3)], turned_recv.at[w])

        @pl.when(jnp.logical_not(inner))
        def _():
            took(old_one.at[pl.ds(0, 4)], turned_recv.at[w])

        fetch(turned_in.at[w], scaled)
        first_fix = 1.0 - beta_one**step_count
        second_fix = 1.0 - beta_two**step_count
        for t in range(4):

            def body(i):
                at = within(i * 8, 8)
                value = scaled[t, at, :]
                new_one = beta_one * one[t, at, :] + (1.0 - beta_one) * value
                new_two = beta_two * two[t, at, :] + (1.0 - beta_two) * value * value
                one[t, at, :] = new_one
                two[t, at, :] = new_two
                scaled[t, at, :] = (
                    new_one / first_fix / (jnp.sqrt(new_two / second_fix) + epsilon)
                )

            loop(rows // 8, body)
            give(
                scaled.at[t],
                scaled_in.at[w, b, within(zin * rows, rows)],
                scaled_send.at[w, t],
                scaled_recv.at[w],
                (y, t, z),
            )

        @pl.when(jnp.logical_not(inner))
        def _():
            plane_scaled(w)
            hop(scaled_part(w), 4 + w)

        fetch(one, one_out.at[slots])
        fetch(two, two_out.at[slots])

    def pull(w):
        plane_scaled(w)
        took(scaled_part(w), hop_recv.at[4 + w])
        fetch_all(
            [(scaled_in.at[w, t], load.at[pl.ds(t * pair, pair)]) for t in range(4)],
            scaled_in.at[w],
        )

        def by_rows(t):
            at = within(t * pair, pair, 16)
            high, low = halves(load[at, :])
            p_hi[at, :] = high
            p_lo[at, :] = low

        loop(4, by_rows)
        for m in range(2):
            at = pl.ds(m * band, band)

            def body(n):
                spot = within(n * tile, tile, tile)
                high, low = halves(
                    triple((p_hi[at, :], p_lo[at, :]), (r_hi[w, :, spot], r_lo[w, :, spot]), PLAIN)
                )
                gq_hi[at, spot] = high
                gq_lo[at, spot] = low

            loop(tiles, body)

    def mirrored(w, t):
        return update.at[w, 0, pl.ds(t * pair, pair)]

    def drain_update(w):
        for t in range(4):
            took(mirrored(w, t), update_send.at[w, t])
            for v in range(2):
                took(update.at[w, 1, pl.ds(0, rows)], final_send.at[2, w, t, v])

    def back(w):
        own_rows = pl.ds(0, 2 * band)
        for slot, side in ((0, 1 - h), (1, h)):
            for m in range(2):
                at = pl.ds(m * band, band)
                spots = [within(t * band + side * pair, pair, 16) for t in (2 * m, 2 * m + 1)]

                def body(n):
                    spot = within(n * tile, tile, tile)
                    own = [
                        jnp.concatenate([turned[w, one_spot, :] for one_spot in spots], axis=0)
                        for turned in (lt_hi, lt_lo)
                    ]
                    update[w, slot, at, spot] = triple(own, (gq_hi[own_rows, spot], gq_lo[own_rows, spot]), PLAIN)

                loop(tiles, body)
                if slot == 0:
                    for t in (2 * m, 2 * m + 1):
                        copy(
                            mirrored(w, t),
                            update_in.at[w, t],
                            update_send.at[w, t],
                            update_recv.at[w, t],
                            (y, b, 3 - z),
                        ).start()

    def finish(w):
        for t in range(4):
            took(update_in.at[w, t], update_recv.at[w, t])
            at = pl.ds(t * pair, pair)
            fetch(update_in.at[w, t], load.at[at])
            update[w, 1, at] = update[w, 1, at] + load[at, :]
            for v in range(2):
                give(
                    update.at[w, 1, pl.ds(t * pair + v * rows, rows)],
                    update_out.at[4 * w + b],
                    final_send.at[2, w, t, v],
                    final_recv.at[2],
                    (y, t, 2 * h + v),
                )

    gather_gradients()

    @pl.when(inner)
    def _():
        mirror_stage(CHUNKS - 1)
        for s in (CHUNKS - 2, CHUNKS - 1):
            pick_stage(s)
        prepare_left(0)
        for s in (CHUNKS - 2, CHUNKS - 1):
            drain_pick(s)
        took(full_grad.at[:, pl.ds(0, 7)], pick_recv.at[0])
        prepare(0)
        turn(0)
        prepare_right(0)
        rotate(0)
        right_product(0)
        left_product(0)
        prepare(1)
        drain_turned(0)
        send_right_product(0)
        prepare_left(1)
        turn(1)

    @pl.when(jnp.logical_not(inner))
    def _():
        edge_right(1)
        edge_left(1)

    moments(0)

    @pl.when(inner)
    def _():
        prepare_right(1)
        rotate(1)
        send_left_product(0)
        right_product(1)
        left_product(1)
        pull(0)
        back(0)

    moments(1)

    @pl.when(inner)
    def _():
        send_right_product(1)
        send_left_product(1)
        pull(1)
        back(1)
        finish(0)
        finish(1)
        drain_left_product(0)
        drain_right_product(0)
        drain_left_product(1)
        drain_right_product(1)
        drain_update(0)
        drain_update(1)
        for s in range(CHUNKS):
            took(pieces.at[s, :, h], mirror_send.at[s])
        for w in range(2):
            for part in range(2):
                took(relay_place(w, part), relay_send.at[w, part])
        took(left.at[pl.ds(0, 6)], final_recv.at[0])
        took(right.at[pl.ds(0, 6)], final_recv.at[1])
        took(old_one.at[pl.ds(0, 6)], final_recv.at[2])

    @pl.when(jnp.logical_not(inner))
    def _():
        for w in range(2):
            took(left_part(w), hop_send.at[w])
            took(right_part(w), hop_send.at[2 + w])
            took(scaled_part(w), hop_send.at[4 + w])
        for s in range(CHUNKS):
            took(band_part(s), hop_send.at[6 + s])
        took(left, final_recv.at[0])
        took(right, final_recv.at[1])
        took(old_one, final_recv.at[2])

    for s in range(CHUNKS):
        took(cross.at[s], cross_send.at[s])


def waved(
    grad_parts,
    master,
    owner_map,
    left_factor,
    right_factor,
    left_basis,
    right_basis,
    moment_one,
    moment_two,
):
    _, source = slot_table(owner_map, lax.axis_size("shard"))
    places = jnp.stack((source // 4, source % 4 // 2, source % 2))
    slots, rows, height = left_basis.shape
    width = right_basis.shape[1]
    cols, half, band, pair, wide = width // 16, width // 2, 4 * rows, 2 * rows, width // 8
    f32, bf16 = jnp.float32, jnp.bfloat16
    right_turned = jnp.swapaxes(right_basis, 1, 2)
    grad = grad_parts[0, 0, 0].reshape(4, band, width)

    def array(*shape):
        return jax.ShapeDtypeStruct(shape, f32)

    def twice(*shape):
        return [pltpu.VMEM(shape, bf16)] * 2

    sems = [
        (CHUNKS,),
        (CHUNKS,),
        (CHUNKS, 4),
        (CHUNKS,),
        (CHUNKS,),
        (CHUNKS,),
        (2, 2, 4, 2),
        (1,),
        (2, 4),
        (2,),
        (2, 4),
        (2,),
        (2, 2),
        (2, 2),
        (2, 4, 2),
        (2,),
        (2, 4),
        (2,),
        (6 + CHUNKS,),
        (6 + CHUNKS,),
        (2, 4),
        (2, 4),
        (3, 2, 4, 2),
        (3,),
    ]
    products = 6 * 2 * 2 * height * height * width
    results = pl.pallas_call(
        banded,
        out_shape=[
            array(slots, rows, height),
            array(slots, cols, width),
            array(slots, rows, width),
            array(slots, rows, width),
            array(slots, rows, width),
            array(CHUNKS, 4, band // CHUNKS, half),
            array(CHUNKS, 4, 2, 2, band // CHUNKS, half),
            array(2, 8, band, half),
            array(2, 4, pair, height),
            array(2, 4, 2, wide, width),
            array(2, 4, rows, width),
            array(2, 4, pair, width),
            array(2, 4, pair, width),
        ],
        in_specs=[
            pl.BlockSpec(memory_space=pl.ANY),
            pl.BlockSpec(memory_space=pltpu.SMEM),
        ]
        + [pl.BlockSpec(memory_space=pl.ANY)] * 4,
        out_specs=[pl.BlockSpec(memory_space=pl.ANY)] * 13,
        scratch_shapes=[
            pltpu.VMEM((4, band // CHUNKS, half), f32),
            pltpu.VMEM((4, 2, 2, band // CHUNKS, half), f32),
            pltpu.VMEM((height, width), f32),
            pltpu.VMEM((2 * band, height), f32),
            *twice(2, height, half),
            *twice(max(4 * wide, 2 * band), max(height, width)),
            *twice(2 * band, height),
            *twice(2, height, 2 * band),
            *twice(2, width, width),
            *twice(2 * band, width),
            pltpu.VMEM((2, 2, 2 * band, width), f32),
            pltpu.VMEM((2, 2 * band, height), f32),
            pltpu.VMEM((2, 4 * wide, width), f32),
            pltpu.VMEM((4, rows, width), f32),
            pltpu.VMEM((4, rows, width), f32),
            pltpu.VMEM((4, rows, width), f32),
            pltpu.SemaphoreType.DMA(()),
        ]
        + [pltpu.SemaphoreType.DMA(shape) for shape in sems],
        compiler_params=pltpu.CompilerParams(
            collective_id=0, has_side_effects=True, vmem_limit_bytes=60 << 20
        ),
        cost_estimate=pl.CostEstimate(flops=products, bytes_accessed=height * width * 80, transcendentals=0),
    )(grad, places, left_basis, right_turned, moment_one, moment_two)
    left_product, right_product, update, new_moment_one, new_moment_two = results[:5]
    new_left = beta_two * left_factor + (1.0 - beta_two) * left_product
    new_right = beta_two * right_factor + (1.0 - beta_two) * right_product
    update_dir = jnp.swapaxes(update, 0, 1)
    new_master = master - learn_rate * (update_dir + decay_weight * master)
    return (new_master, update_dir, new_left, new_right, new_moment_one, new_moment_two)


def solution(mesh):
    shards, tensors, sections = (mesh.shape[name] for name in ("shard", "tensor", "section"))

    def run(*operands):
        own = operands[3].shape[0] // shards
        paired = (shards, tensors, sections, own) == (2, 4, 4, 8)
        band = ("tensor", "section")
        placed = (
            P("shard", "tensor", "section", None, None),
            P(band, "shard", None),
            P(),
            P("shard", band, None),
            P("shard", band, None),
            P("shard", band, None),
            P("shard", None, band),
            P("shard", band, None),
            P("shard", band, None),
        )
        results = (placed[1], placed[1], placed[3], placed[4], placed[7], placed[8])
        return jax.shard_map(
            waved if paired else local,
            mesh=mesh,
            in_specs=placed,
            out_specs=results,
            check_vma=False,
        )(*operands)

    return run
```

```python
import jax
import jax.numpy as jnp
from jax import lax
from jax.experimental import pallas as pl
from jax.experimental.pallas import tpu as pltpu
from jax.sharding import PartitionSpec as P

beta_one = 0.95
beta_two = 0.95
epsilon = 1e-08
learn_rate = 0.01
decay_weight = 0.1
step_count = 10


def slot_table(owner_map, shards):
    owners_flat = owner_map.reshape(-1)
    matrices = owners_flat.shape[0]
    per_owner = matrices // shards
    member = (owners_flat[:, None] == jnp.arange(shards, dtype=jnp.int32)[None, :]).astype(
        jnp.int32
    )
    order = jnp.arange(matrices, dtype=jnp.int32)
    earlier = (order[:, None] > order[None, :]).astype(jnp.int32)
    before = jnp.sum(earlier[:, :, None] * member[None, :, :], axis=1)
    rank_in = jnp.sum(before * member, axis=1)
    slot_of = owners_flat * per_owner + rank_in
    places = (slot_of[:, None] == jnp.arange(matrices, dtype=jnp.int32)[None, :]).astype(jnp.int32)
    source = jnp.sum(places * jnp.arange(matrices, dtype=jnp.int32)[:, None], axis=0)
    return (slot_of, source)


def pick(stacked, indices):
    return jnp.stack(
        [
            lax.dynamic_index_in_dim(stacked, indices[i], 0, keepdims=False)
            for i in range(indices.shape[0])
        ]
    )


def local(
    grad_parts,
    master,
    owner_map,
    left_factor,
    right_factor,
    left_basis,
    right_basis,
    moment_one,
    moment_two,
):
    exact_mode = lax.Precision.HIGHEST
    shards = lax.axis_size("shard")
    members = lax.axis_size(("tensor", "section"))
    position = lax.axis_index(("tensor", "section"))
    slot_of, source = slot_table(owner_map, shards)
    height = left_basis.shape[2]
    width = right_basis.shape[1]
    row_block = height // members
    col_block = width // members
    local_part = grad_parts[0, 0, 0]
    row_piece = lax.psum_scatter(local_part, "shard", scatter_dimension=0, tiled=True)
    stacked = lax.all_gather(row_piece[None], ("tensor", "section"), axis=0, tiled=True)
    ordered = pick(stacked, source)
    full_grad = lax.all_to_all(ordered, "shard", split_axis=0, concat_axis=1, tiled=True)
    full_right = lax.all_gather(right_basis, ("tensor", "section"), axis=2, tiled=True)
    grad_band = lax.dynamic_slice_in_dim(full_grad, position * row_block, row_block, 1)
    grad_slab = lax.dynamic_slice_in_dim(full_grad, position * col_block, col_block, 2)
    new_left = beta_two * left_factor + (1.0 - beta_two) * jnp.einsum(
        "orn,ofn->orf", grad_band, full_grad, precision=exact_mode
    )
    new_right = beta_two * right_factor + (1.0 - beta_two) * jnp.einsum(
        "ofc,ofn->ocn", grad_slab, full_grad, precision=exact_mode
    )
    turned = jnp.einsum("orf,ofn->orn", left_basis, full_grad, precision=exact_mode)
    rotated = jnp.einsum("orn,onk->ork", turned, full_right, precision=exact_mode)
    new_moment_one = beta_one * moment_one + (1.0 - beta_one) * rotated
    new_moment_two = beta_two * moment_two + (1.0 - beta_two) * rotated * rotated
    first_fix = 1.0 - beta_one**step_count
    second_fix = 1.0 - beta_two**step_count
    scaled = new_moment_one / first_fix / (jnp.sqrt(new_moment_two / second_fix) + epsilon)
    pulled = jnp.einsum("orn,okn->ork", scaled, full_right, precision=exact_mode)
    update_dir = lax.psum_scatter(
        jnp.einsum("orf,ork->fok", left_basis, pulled, precision=exact_mode),
        ("tensor", "section"),
        scatter_dimension=0,
        tiled=True,
    )
    new_master = master - learn_rate * (update_dir + decay_weight * master)
    return (new_master, update_dir, new_left, new_right, new_moment_one, new_moment_two)


def halves(value):
    high = value.astype(jnp.bfloat16)
    return high, (value - high.astype(jnp.float32)).astype(jnp.bfloat16)


def triple(first, second, contract):
    def one(a, b):
        return lax.dot_general(a, b, (contract, ((), ())), preferred_element_type=jnp.float32)

    (a, a_low), (b, b_low) = first, second
    return one(a, b) + (one(a, b_low) + one(a_low, b))


PLAIN = ((1,), (0,))
TURNED = ((1,), (1,))
CHUNKS = 6


def banded(
    grad,
    source,
    left,
    right,
    old_one,
    old_two,
    left_out,
    right_out,
    update_out,
    one_out,
    two_out,
    cross,
    pieces,
    full_grad,
    left_half,
    right_full,
    turned_in,
    scaled_in,
    update_in,
    crossed,
    piece,
    load,
    load_left,
    g_hi,
    g_lo,
    gq_hi,
    gq_lo,
    l_hi,
    l_lo,
    lt_hi,
    lt_lo,
    r_hi,
    r_lo,
    p_hi,
    p_lo,
    update,
    left_prod,
    right_prod,
    one,
    two,
    scaled,
    local_sem,
    cross_send,
    cross_recv,
    band_send,
    band_recv,
    mirror_send,
    mirror_recv,
    pick_send,
    pick_recv,
    left_send,
    left_recv,
    right_send,
    right_recv,
    relay_send,
    relay_recv,
    turned_send,
    turned_recv,
    scaled_send,
    scaled_recv,
    hop_send,
    hop_recv,
    block_send,
    block_recv,
    update_send,
    update_recv,
    final_send,
    final_recv,
):
    mesh_id = pl.DeviceIdType.MESH
    y, b, z = lax.axis_index("shard"), lax.axis_index("tensor"), lax.axis_index("section")
    h, zin = lax.div(z, 2), lax.rem(z, 2)
    core_z = 1 + h
    inner = (z == 1) | (z == 2)
    rows, height = left.shape[1], left.shape[2]
    cols, width = right.shape[1], right.shape[2]
    half = width // 2
    band = 4 * rows
    step = band // CHUNKS
    pair, wide = 2 * rows, 2 * cols
    tile = min(256, half)
    tiles = width // tile
    tall = 384 if height % 384 == 0 else 128

    def within(start, size, unit=8):
        return pl.ds(pl.multiple_of(start, unit), size)

    def copy(src, dst, send, recv, target):
        return pltpu.make_async_remote_copy(
            src_ref=src,
            dst_ref=dst,
            send_sem=send,
            recv_sem=recv,
            device_id=target,
            device_id_type=mesh_id,
        )

    def give(src, dst, send, recv, target):
        here = (target[0] == y) & (target[1] == b) & (target[2] == z)

        @pl.when(here)
        def _():
            pltpu.make_async_copy(src, dst, send).start()

        @pl.when(jnp.logical_not(here))
        def _():
            copy(src, dst, send, recv, target).start()

    def took(ref, sem):
        pltpu.make_async_copy(ref, ref, sem).wait()

    def fetch(src, dst):
        moved = pltpu.make_async_copy(src, dst, local_sem)
        moved.start()
        moved.wait()

    def fetch_all(moves, whole):
        for src, dst in moves:
            pltpu.make_async_copy(src, dst, local_sem).start()
        took(whole, local_sem)

    def loop(count, body):
        def run(i, carry):
            body(i)
            return carry

        lax.fori_loop(0, count, run, 0)

    barrier = pltpu.get_barrier_semaphore()
    for dy in range(2):
        for db in range(4):
            for dz in range(2):
                if dy or db or dz:
                    other = (
                        lax.rem(y + dy, 2),
                        lax.rem(b + db, 4),
                        2 * h + lax.rem(zin + dz, 2),
                    )
                    pl.semaphore_signal(barrier, inc=1, device_id=other, device_id_type=mesh_id)

    @pl.when(inner)
    def _():
        pl.semaphore_signal(barrier, inc=1, device_id=(y, b, 3 - z), device_id_type=mesh_id)
        pl.semaphore_wait(barrier, 16)

    @pl.when(jnp.logical_not(inner))
    def _():
        pl.semaphore_wait(barrier, 15)

    def lanes(side):
        return within(side * half, half, 128)

    for s in range(CHUNKS):
        copy(
            grad.at[:, pl.ds(s * step, step), lanes(1 - y)],
            cross.at[s],
            cross_send.at[s],
            cross_recv.at[s],
            (1 - y, b, z),
        ).start()

    def send_right(w):
        for t in range(4):
            give(
                right.at[4 * w + t],
                right_full.at[w, b, h, within(zin * cols, cols)],
                right_send.at[w, t],
                right_recv.at[w],
                (y, t, z),
            )

    def send_left(w):
        for t in range(4):
            give(
                left.at[4 * w + t],
                left_half.at[w, b, within(zin * rows, rows)],
                left_send.at[w, t],
                left_recv.at[w],
                (y, t, z),
            )

    def drain_right(w):
        for t in range(4):
            took(right.at[0], right_send.at[w, t])

    def drain_left(w):
        for t in range(4):
            took(left.at[0], left_send.at[w, t])

    def drain_bands(s):
        for t in range(4):
            took(crossed.at[t], band_send.at[s, t])

    def drain_scaled(w):
        for t in range(4):
            took(scaled.at[t], scaled_send.at[w, t])

    def hop(place, n):
        copy(place, place, hop_send.at[n], hop_recv.at[n], (y, b, core_z)).start()

    def left_part(w):
        return left_half.at[w, :, within(zin * rows, rows)]

    def right_part(w):
        return right_full.at[w, :, h, within(zin * cols, cols)]

    def band_part(s):
        return pieces.at[s, :, h, zin]

    def plane_left(w):
        drain_left(w)
        took(left.at[pl.ds(0, 3)], left_recv.at[w])

    def plane_right(w):
        drain_right(w)
        took(right.at[pl.ds(0, 3)], right_recv.at[w])

    def plane_bands(s):
        drain_bands(s)
        took(crossed.at[pl.ds(0, 3)], band_recv.at[s])

    def plane_scaled(w):
        drain_scaled(w)
        for k in range(1, 4):
            took(scaled.at[0], scaled_recv.at[w, lax.rem(b + k, 4)])

    def relay_place(w, part):
        v = zin if part == 0 else 1 - zin
        return right_full.at[w, :, h, within(v * cols, cols)]

    def relay_right(w, part):
        place = relay_place(w, part)
        copy(
            place, place, relay_send.at[w, part], relay_recv.at[w, part], (y, b, 3 - z)
        ).start()

    def relay_hop(w):
        took(right_part(w), hop_recv.at[2 + w])
        relay_right(w, 1)

    def sum_ref(s):
        holder = (one, two, scaled)[s // 2 % 3]
        return holder.at[:, pl.ds(0, step), pl.ds(s % 2 * half, half)]

    def sum_stage(s):
        part = sum_ref(s)
        fetch(grad.at[:, pl.ds(s * step, step), lanes(y)], part)
        took(cross.at[s], cross_recv.at[s])
        fetch(cross.at[s], crossed)
        part[...] = part[...] + crossed[...]
        for t in range(4):
            give(
                part.at[t],
                pieces.at[s, b, h, zin],
                band_send.at[s, t],
                band_recv.at[s],
                (y, t, z),
            )

    def mirror_stage(s):
        plane_bands(s)
        took(band_part(s), hop_recv.at[4 + s])
        copy(
            pieces.at[s, :, h],
            pieces.at[s, :, h],
            mirror_send.at[s],
            mirror_recv.at[s],
            (y, b, 3 - z),
        ).start()

    def staged(s, o, t, w):
        return update.at[0, s % 2, pl.ds((4 * o + t) * step, step), pl.ds(w * half, half)]

    def drain_pick(s):
        for o in range(2):
            for t in range(4):
                for w in range(2):
                    took(staged(s, o, t, w), pick_send.at[s % 2, o, t, w])

    def pick_stage(s):
        took(pieces.at[s, :, 1 - h], mirror_recv.at[s])
        if s == CHUNKS - 1:
            relay_hop(0)
            relay_right(1, 0)
            relay_hop(1)
        fetch(pieces.at[s], piece)
        if s >= 2:
            drain_pick(s - 2)
        for o in range(2):
            for t in range(4):
                for w in range(2):
                    at = 8 * o + 4 * w + t
                    block = staged(s, o, t, w)
                    block[...] = piece[source[0, at], source[1, at], source[2, at]]
                    give(
                        block,
                        full_grad.at[w, 4 * y + b, pl.ds(s * step, step)],
                        pick_send.at[s % 2, o, t, w],
                        pick_recv.at[0],
                        (o, t, z),
                    )

    def edge(body):
        pl.when(jnp.logical_not(inner))(body)

    def edge_right(w):
        plane_right(w)
        hop(right_part(w), 2 + w)

    def edge_left(w):
        plane_left(w)
        hop(left_part(w), w)

    def gather_gradients():
        send_right(0)
        for s in range(CHUNKS):
            sum_stage(s)

            @pl.when(jnp.logical_not(inner))
            def _():
                plane_bands(s)
                hop(band_part(s), 4 + s)
                if s == 1:
                    edge_right(0)
                if s == 3:
                    edge_left(0)

            if s == 0:
                send_left(0)
            if s == 1:
                send_right(1)
            if s == 2:
                send_left(1)

            @pl.when(inner)
            def _():
                if s == 0:
                    plane_right(0)
                    relay_right(0, 0)
                if s == 4:
                    plane_right(1)
                if s >= 1:
                    mirror_stage(s - 1)
                if s >= 2:
                    pick_stage(s - 2)

    def load_grad(w):
        fetch_all(
            [
                (
                    full_grad.at[w, 4 * side + t],
                    load.at[pl.ds(t * band, band), pl.ds(side * half, half)],
                )
                for side in range(2)
                for t in range(4)
            ],
            full_grad.at[w],
        )

    def prepare(w):
        load_grad(w)

        def by_rows(i):
            at = within(i * pair, pair, 16)
            high, low = halves(load[at, :])
            for side in range(2):
                g_hi[side, at, :] = high[:, side * half : (side + 1) * half]
                g_lo[side, at, :] = low[:, side * half : (side + 1) * half]

        loop(8, by_rows)

    def prepare_turned():
        def by_columns(t):
            own = load[pl.ds(0, height), within((2 * t + h) * wide, wide, wide)]
            high, low = halves(own.T)
            at = within(t * wide, wide, 16)
            gq_hi[at, pl.ds(0, height)] = high
            gq_lo[at, pl.ds(0, height)] = low

        loop(4, by_columns)

    def prepare_left(w):
        plane_left(w)
        took(left_part(w), hop_recv.at[w])
        fetch_all(
            [(left_half.at[w, t], load_left.at[pl.ds(t * pair, pair)]) for t in range(4)],
            left_half.at[w],
        )

        def by_rows(t):
            at = within(t * pair, pair, 16)
            high, low = halves(load_left[at, :])
            l_hi[at, :] = high
            l_lo[at, :] = low

        loop(4, by_rows)

        def by_columns(i):
            at = within(i * 128, 128, 128)
            high, low = halves(load_left[:, at].T)
            lt_hi[w, at, :] = high
            lt_lo[w, at, :] = low

        loop(height // 128, by_columns)

    def prepare_right(w):
        for part in range(2):
            took(relay_place(w, part), relay_recv.at[w, part])
        fetch_all(
            [
                (right_full.at[w, t, v], load.at[pl.ds((2 * t + v) * wide, wide)])
                for t in range(4)
                for v in range(2)
            ],
            right_full.at[w],
        )

        def by_rows(i):
            at = within(i * wide, wide, 16)
            high, low = halves(load[at, :])
            r_hi[w, at, :] = high
            r_lo[w, at, :] = low

        loop(8, by_rows)

    def turn(w):
        for m in range(2):
            at = pl.ds(m * band, band)

            def body(n):
                side, spot = n // (tiles // 2), within(n % (tiles // 2) * tile, tile, tile)
                product = triple(
                    (l_hi[at, :], l_lo[at, :]),
                    (g_hi[side, :, spot], g_lo[side, :, spot]),
                    PLAIN,
                )
                high, low = halves(product)
                into = within(n * tile, tile, tile)
                p_hi[at, into] = high
                p_lo[at, into] = low

            loop(tiles, body)

    def rotated(t, v):
        return load_left.at[pl.ds(t * pair + v * rows, rows), pl.ds(0, width)]

    def drain_turned(w):
        for t in range(4):
            for v in range(2):
                took(rotated(t, v), turned_send.at[w, t, v])

    def rotate(w):
        for m in range(2):
            at = pl.ds(m * band, band)

            def body(n):
                spot = within(n * tile, tile, tile)
                load_left[at, spot] = triple(
                    (p_hi[at, :], p_lo[at, :]), (r_hi[w, spot, :], r_lo[w, spot, :]), TURNED
                )

            loop(tiles, body)
            for t in (2 * m, 2 * m + 1):
                for v in range(2):
                    give(
                        rotated(t, v),
                        turned_in.at[w, b],
                        turned_send.at[w, t, v],
                        turned_recv.at[w],
                        (y, t, 2 * h + v),
                    )

    def drain_left_product(w):
        for t in range(4):
            for v in range(2):
                took(left_prod.at[w, pl.ds(0, rows)], final_send.at[0, w, t, v])

    def drain_right_product(w):
        for t in range(4):
            for v in range(2):
                took(right_prod.at[w, pl.ds(0, cols)], final_send.at[1, w, t, v])

    def left_product(w):
        for m in range(2):
            at = pl.ds(m * band, band)
            spots = [within(t * band + h * pair, pair, 16) for t in (2 * m, 2 * m + 1)]

            def body(n):
                spot = within(n * tall, tall, 128)
                total = None
                for side in range(2):
                    own = [
                        jnp.concatenate([g[side, one_spot, :] for one_spot in spots], axis=0)
                        for g in (g_hi, g_lo)
                    ]
                    product = triple(own, (g_hi[side, spot, :], g_lo[side, spot, :]), TURNED)
                    total = product if total is None else total + product
                left_prod[w, at, spot] = total

            loop(height // tall, body)

    def send_left_product(w):
        for t in range(4):
            for v in range(2):
                give(
                    left_prod.at[w, pl.ds(t * pair + v * rows, rows)],
                    left_out.at[4 * w + b],
                    final_send.at[0, w, t, v],
                    final_recv.at[0],
                    (y, t, 2 * h + v),
                )

    def right_product(w):
        for m in range(2):
            at = pl.ds(m * 2 * wide, 2 * wide)

            def body(n):
                side, spot = n // (tiles // 2), within(n % (tiles // 2) * tile, tile, tile)
                right_prod[w, at, within(n * tile, tile, tile)] = triple(
                    (gq_hi[at, pl.ds(0, height)], gq_lo[at, pl.ds(0, height)]),
                    (g_hi[side, :, spot], g_lo[side, :, spot]),
                    PLAIN,
                )

            loop(tiles, body)

    def send_right_product(w):
        for t in range(4):
            for v in range(2):
                give(
                    right_prod.at[w, pl.ds(t * wide + v * cols, cols)],
                    right_out.at[4 * w + b],
                    final_send.at[1, w, t, v],
                    final_recv.at[1],
                    (y, t, 2 * h + v),
                )

    def moments(w):
        slots = pl.ds(4 * w, 4)
        fetch_all([(old_one.at[slots], one)], one)
        fetch_all([(old_two.at[slots], two)], two)

        @pl.when(inner)
        def _():
            if w:
                drain_turned(w)
            took(old_one.at[pl.ds(0, 3)], turned_recv.at[w])

        @pl.when(jnp.logical_not(inner))
        def _():
            took(old_one.at[pl.ds(0, 4)], turned_recv.at[w])

        fetch(turned_in.at[w], scaled)
        first_fix = 1.0 - beta_one**step_count
        second_fix = 1.0 - beta_two**step_count
        for t in range(4):

            def body(i):
                at = within(i * 8, 8)
                value = scaled[t, at, :]
                new_one = beta_one * one[t, at, :] + (1.0 - beta_one) * value
                new_two = beta_two * two[t, at, :] + (1.0 - beta_two) * value * value
                one[t, at, :] = new_one
                two[t, at, :] = new_two
                scaled[t, at, :] = (
                    new_one / first_fix / (jnp.sqrt(new_two / second_fix) + epsilon)
                )

            loop(rows // 8, body)
            give(
                scaled.at[t],
                scaled_in.at[w, b, within(zin * rows, rows)],
                scaled_send.at[w, t],
                scaled_recv.at[w, b],
                (y, t, z),
            )

        @pl.when(jnp.logical_not(inner))
        def _():
            for k in range(4):
                t = lax.rem(b + k, 4)
                arrived = scaled_send if k == 0 else scaled_recv
                took(scaled.at[0], arrived.at[w, t])
                place = scaled_in.at[w, t, within(zin * rows, rows)]
                copy(
                    place, place, block_send.at[w, t], block_recv.at[w, t], (y, b, core_z)
                ).start()
            for k in range(1, 4):
                took(scaled.at[0], scaled_send.at[w, lax.rem(b + k, 4)])

        fetch(one, one_out.at[slots])
        fetch(two, two_out.at[slots])

    def pull(w):
        plane_scaled(w)
        for t in range(4):
            took(scaled.at[0], block_recv.at[w, t])
        fetch_all(
            [(scaled_in.at[w, t], load.at[pl.ds(t * pair, pair)]) for t in range(4)],
            scaled_in.at[w],
        )

        def by_rows(t):
            at = within(t * pair, pair, 16)
            high, low = halves(load[at, :])
            p_hi[at, :] = high
            p_lo[at, :] = low

        loop(4, by_rows)
        for m in range(2):
            at = pl.ds(m * band, band)

            def body(n):
                spot = within(n * tile, tile, tile)
                high, low = halves(
                    triple((p_hi[at, :], p_lo[at, :]), (r_hi[w, :, spot], r_lo[w, :, spot]), PLAIN)
                )
                gq_hi[at, spot] = high
                gq_lo[at, spot] = low

            loop(tiles, body)

    def mirrored(w, t):
        return update.at[w, 0, pl.ds(t * pair, pair)]

    def drain_update(w):
        for t in range(4):
            took(mirrored(w, t), update_send.at[w, t])
            for v in range(2):
                took(update.at[w, 1, pl.ds(0, rows)], final_send.at[2, w, t, v])

    def back(w):
        own_rows = pl.ds(0, 2 * band)
        for slot, side in ((0, 1 - h), (1, h)):
            for m in range(2):
                at = pl.ds(m * band, band)
                spots = [within(t * band + side * pair, pair, 16) for t in (2 * m, 2 * m + 1)]

                def body(n):
                    spot = within(n * tile, tile, tile)
                    own = [
                        jnp.concatenate([turned[w, one_spot, :] for one_spot in spots], axis=0)
                        for turned in (lt_hi, lt_lo)
                    ]
                    update[w, slot, at, spot] = triple(own, (gq_hi[own_rows, spot], gq_lo[own_rows, spot]), PLAIN)

                loop(tiles, body)
                if slot == 0:
                    for t in (2 * m, 2 * m + 1):
                        copy(
                            mirrored(w, t),
                            update_in.at[w, t],
                            update_send.at[w, t],
                            update_recv.at[w, t],
                            (y, b, 3 - z),
                        ).start()

    def finish(w):
        for t in range(4):
            took(update_in.at[w, t], update_recv.at[w, t])
            at = pl.ds(t * pair, pair)
            fetch(update_in.at[w, t], load.at[at])
            update[w, 1, at] = update[w, 1, at] + load[at, :]
            for v in range(2):
                give(
                    update.at[w, 1, pl.ds(t * pair + v * rows, rows)],
                    update_out.at[4 * w + b],
                    final_send.at[2, w, t, v],
                    final_recv.at[2],
                    (y, t, 2 * h + v),
                )

    gather_gradients()

    @pl.when(inner)
    def _():
        mirror_stage(CHUNKS - 1)
        for s in (CHUNKS - 2, CHUNKS - 1):
            pick_stage(s)
        prepare_left(0)
        for s in (CHUNKS - 2, CHUNKS - 1):
            drain_pick(s)
        took(full_grad.at[:, pl.ds(0, 7)], pick_recv.at[0])
        prepare(0)
        turn(0)
        prepare_right(0)
        rotate(0)
        load_grad(0)
        prepare_turned()
        right_product(0)
        left_product(0)
        prepare(1)
        prepare_turned()
        drain_turned(0)
        send_right_product(0)
        prepare_left(1)
        turn(1)

    @pl.when(jnp.logical_not(inner))
    def _():
        edge_right(1)
        edge_left(1)

    moments(0)

    @pl.when(inner)
    def _():
        prepare_right(1)
        rotate(1)
        send_left_product(0)
        right_product(1)
        left_product(1)
        pull(0)
        back(0)

    moments(1)

    @pl.when(inner)
    def _():
        send_right_product(1)
        send_left_product(1)
        pull(1)
        back(1)
        finish(0)
        finish(1)
        drain_left_product(0)
        drain_right_product(0)
        drain_left_product(1)
        drain_right_product(1)
        drain_update(0)
        drain_update(1)
        for s in range(CHUNKS):
            took(pieces.at[s, :, h], mirror_send.at[s])
        for w in range(2):
            for part in range(2):
                took(relay_place(w, part), relay_send.at[w, part])
        took(left.at[pl.ds(0, 6)], final_recv.at[0])
        took(right.at[pl.ds(0, 6)], final_recv.at[1])
        took(old_one.at[pl.ds(0, 6)], final_recv.at[2])

    @pl.when(jnp.logical_not(inner))
    def _():
        for w in range(2):
            took(left_part(w), hop_send.at[w])
            took(right_part(w), hop_send.at[2 + w])
            for t in range(4):
                took(scaled.at[0], block_send.at[w, t])
        for s in range(CHUNKS):
            took(band_part(s), hop_send.at[4 + s])
        took(left, final_recv.at[0])
        took(right, final_recv.at[1])
        took(old_one, final_recv.at[2])

    for s in range(CHUNKS):
        took(cross.at[s], cross_send.at[s])


def finished(update, master, left_factor, left_product, new_master, update_dir, new_left):
    for q in range(update.shape[0]):
        update_dir[:, q, :] = update[q]
    turned = update_dir[...]
    old = master[...]
    new_master[...] = old - learn_rate * (turned + decay_weight * old)
    new_left[...] = beta_two * left_factor[...] + (1.0 - beta_two) * left_product[...]


def waved(
    grad_parts,
    master,
    owner_map,
    left_factor,
    right_factor,
    left_basis,
    right_basis,
    moment_one,
    moment_two,
):
    _, source = slot_table(owner_map, lax.axis_size("shard"))
    places = jnp.stack((source // 4, source % 4 // 2, source % 2))
    slots, rows, height = left_basis.shape
    width = right_basis.shape[1]
    cols, half, band, pair, wide = width // 16, width // 2, 4 * rows, 2 * rows, width // 8
    f32, bf16 = jnp.float32, jnp.bfloat16
    right_turned = jnp.swapaxes(right_basis, 1, 2)
    grad = grad_parts[0, 0, 0].reshape(4, band, width)

    def array(*shape):
        return jax.ShapeDtypeStruct(shape, f32)

    def twice(*shape):
        return [pltpu.VMEM(shape, bf16)] * 2

    sems = [
        (CHUNKS,),
        (CHUNKS,),
        (CHUNKS, 4),
        (CHUNKS,),
        (CHUNKS,),
        (CHUNKS,),
        (2, 2, 4, 2),
        (1,),
        (2, 4),
        (2,),
        (2, 4),
        (2,),
        (2, 2),
        (2, 2),
        (2, 4, 2),
        (2,),
        (2, 4),
        (2, 4),
        (4 + CHUNKS,),
        (4 + CHUNKS,),
        (2, 4),
        (2, 4),
        (2, 4),
        (2, 4),
        (3, 2, 4, 2),
        (3,),
    ]
    products = 6 * 2 * 2 * height * height * width
    results = pl.pallas_call(
        banded,
        out_shape=[
            array(slots, rows, height),
            array(slots, cols, width),
            array(slots, rows, width),
            array(slots, rows, width),
            array(slots, rows, width),
            array(CHUNKS, 4, band // CHUNKS, half),
            array(CHUNKS, 4, 2, 2, band // CHUNKS, half),
            array(2, 8, band, half),
            array(2, 4, pair, height),
            array(2, 4, 2, wide, width),
            array(2, 4, rows, width),
            array(2, 4, pair, width),
            array(2, 4, pair, width),
        ],
        in_specs=[
            pl.BlockSpec(memory_space=pl.ANY),
            pl.BlockSpec(memory_space=pltpu.SMEM),
        ]
        + [pl.BlockSpec(memory_space=pl.ANY)] * 4,
        out_specs=[pl.BlockSpec(memory_space=pl.ANY)] * 13,
        scratch_shapes=[
            pltpu.VMEM((4, band // CHUNKS, half), f32),
            pltpu.VMEM((4, 2, 2, band // CHUNKS, half), f32),
            pltpu.VMEM((height, width), f32),
            pltpu.VMEM((2 * band, height), f32),
            *twice(2, height, half),
            *twice(max(4 * wide, 2 * band), max(height, width)),
            *twice(2 * band, height),
            *twice(2, height, 2 * band),
            *twice(2, width, width),
            *twice(2 * band, width),
            pltpu.VMEM((2, 2, 2 * band, width), f32),
            pltpu.VMEM((2, 2 * band, height), f32),
            pltpu.VMEM((2, 4 * wide, width), f32),
            pltpu.VMEM((4, rows, width), f32),
            pltpu.VMEM((4, rows, width), f32),
            pltpu.VMEM((4, rows, width), f32),
            pltpu.SemaphoreType.DMA(()),
        ]
        + [pltpu.SemaphoreType.DMA(shape) for shape in sems],
        compiler_params=pltpu.CompilerParams(
            collective_id=0, has_side_effects=True, vmem_limit_bytes=60 << 20
        ),
        cost_estimate=pl.CostEstimate(flops=products, bytes_accessed=height * width * 80, transcendentals=0),
    )(grad, places, left_basis, right_turned, moment_one, moment_two)
    left_product, right_product, update, new_moment_one, new_moment_two = results[:5]
    new_right = beta_two * right_factor + (1.0 - beta_two) * right_product

    some = 24 if rows % 24 == 0 else 8
    by_slot = pl.BlockSpec((slots, some, width), lambda i: (0, i, 0))
    by_unit = pl.BlockSpec((some, slots, width), lambda i: (i, 0, 0))
    by_row = pl.BlockSpec((slots, some, height), lambda i: (0, i, 0))
    new_master, update_dir, new_left = pl.pallas_call(
        finished,
        grid=(rows // some,),
        out_shape=[array(rows, slots, width), array(rows, slots, width), array(slots, rows, height)],
        in_specs=[by_slot, by_unit, by_row, by_row],
        out_specs=[by_unit, by_unit, by_row],
        compiler_params=pltpu.CompilerParams(vmem_limit_bytes=32 << 20),
    )(update, master, left_factor, left_product)
    return (new_master, update_dir, new_left, new_right, new_moment_one, new_moment_two)


def solution(mesh):
    shards, tensors, sections = (mesh.shape[name] for name in ("shard", "tensor", "section"))

    def run(*operands):
        own = operands[3].shape[0] // shards
        paired = (shards, tensors, sections, own) == (2, 4, 4, 8)
        band = ("tensor", "section")
        placed = (
            P("shard", "tensor", "section", None, None),
            P(band, "shard", None),
            P(),
            P("shard", band, None),
            P("shard", band, None),
            P("shard", band, None),
            P("shard", None, band),
            P("shard", band, None),
            P("shard", band, None),
        )
        results = (placed[1], placed[1], placed[3], placed[4], placed[7], placed[8])
        return jax.shard_map(
            waved if paired else local,
            mesh=mesh,
            in_specs=placed,
            out_specs=results,
            check_vma=False,
        )(*operands)

    return run
```
